32 devices in a mesh: grp: 2 (over y), wid: 4 (over z), hgt: 4 (over x, core).
Axes of the slice: x: 2, y: 2, z: 4, core: 2. Of those that a mesh axis runs over, the one named last changes fastest.
Arguments:
- latent_query: bfloat16 [8, 16, 32, 1536], P('grp', 'hgt', 'wid'), parts along dimension 0, may hold values from -20 to 20
- latent_key: bfloat16 [8, 16, 32, 1536], P('grp', 'hgt', 'wid'), parts along dimension 0, may hold values from -20 to 20
- latent_value: bfloat16 [8, 16, 32, 1536], P('grp', 'hgt', 'wid'), parts along dimension 0, may hold values from -6 to 6
- latent_grad: bfloat16 [8, 16, 32, 1536], P('grp', 'hgt', 'wid'), parts along dimension 0, may hold values from -6 to 6
- text_query: bfloat16 [256, 1536], P('grp'), parts along dimension 0, may hold values from -20 to 20
- text_key: bfloat16 [256, 1536], P('grp'), parts along dimension 0, may hold values from -20 to 20
- text_value: bfloat16 [256, 1536], P('grp'), parts along dimension 0, may hold values from -6 to 6
- text_grad: bfloat16 [256, 1536], P('grp'), parts along dimension 0, may hold values from -6 to 6
- text_valid: int32 [256], P('grp'), parts along dimension 0, may hold values 0 or 1
- windows: int32 [8, 9], replicated, may hold values from -1 to 7, as said below
Outputs:
- latent_out: bfloat16 [8, 16, 32, 1536], P('grp', 'hgt', 'wid'), parts along dimension 0
- grad_query: bfloat16 [8, 16, 32, 1536], P('grp', 'hgt', 'wid'), parts along dimension 0
- grad_key: bfloat16 [8, 16, 32, 1536], P('grp', 'hgt', 'wid'), parts along dimension 0
- grad_value: bfloat16 [8, 16, 32, 1536], P('grp', 'hgt', 'wid'), parts along dimension 0
- text_out: bfloat16 [256, 1536], P(('grp', 'wid', 'hgt')), parts along dimension 0
- text_grad_query: bfloat16 [256, 1536], P(('grp', 'wid', 'hgt')), parts along dimension 0
- text_grad_key: bfloat16 [256, 1536], P(('grp', 'wid', 'hgt')), parts along dimension 0
- text_grad_value: bfloat16 [256, 1536], P(('grp', 'wid', 'hgt')), parts along dimension 0
The draws below stay inside these ranges and needn't reach their ends.
There are 2 independent parts, one for each index of `grp`. The reference program is written for one: setup_inputs(seed, part) draws one part's arguments, and reference() takes and returns one part's arrays. A program takes and returns all parts, laid end to end along the dimension named above; an argument that names none is the same for every part. Nothing has to cross between parts.
Inputs may be any that keep to these rules, and one draw needn't show every extreme that they name: `windows`: slot s of tile t holds the tile (s // 3 - 1) tile rows and (s % 3 - 1) tile columns away from t, or -1; it holds -1 where that tile lies outside the grid, and slot 4 always holds t. Tiles are numbered row by row, 4 to a row.
All inputs are finite; a program needn't handle non-finite values.
Results may differ from the reference program's by a relative error of at most 0.034.
Values may be sent and summed in bfloat16 or wider, within the bound.
A program may use at most 128 MiB of HBM per device.

```python
import jax
import jax.numpy as jnp
from jax import lax

HEADS = 12
HEAD_DIM = 128
TILE_T = 4
TILE_H = 8
TILE_W = 8
TEXT = 128
GRID_H = 16
GRID_W = 32
TILES = 8


def drawn_values(key, salt, spread, shape):
    noise = jnp.clip(jax.random.normal(jax.random.fold_in(key, salt), shape, jnp.float32), -4.0, 4.0)
    return (spread * noise).astype(jnp.bfloat16)


def draw_latent_query(key, part):
    shape = (TILE_T, GRID_H, GRID_W, HEADS * HEAD_DIM)
    return drawn_values(key, 1, 2.5, shape)


def draw_latent_key(key, part):
    shape = (TILE_T, GRID_H, GRID_W, HEADS * HEAD_DIM)
    return drawn_values(key, 2, 1.0, shape)


def draw_text_query(key, part):
    shape = (TEXT, HEADS * HEAD_DIM)
    return drawn_values(key, 3, 2.5, shape)


def draw_text_key(key, part):
    shape = (TEXT, HEADS * HEAD_DIM)
    return drawn_values(key, 4, 1.0, shape)


def draw_windows(key, part):
    grid_rows = GRID_H // TILE_H
    grid_cols = GRID_W // TILE_W
    count = grid_rows * grid_cols
    tile = jnp.arange(count, dtype=jnp.int32)[:, None]
    slot = jnp.arange(9, dtype=jnp.int32)[None, :]
    near_row = tile // grid_cols + slot // 3 - 1
    near_col = tile % grid_cols + slot % 3 - 1
    inside = (near_row >= 0) & (near_row < grid_rows) & (near_col >= 0) & (near_col < grid_cols)
    keep = (jax.random.randint(key, (count, 9), 0, 3) > 0) | (slot == 4)
    return jnp.where(inside & keep, near_row * grid_cols + near_col, -1).astype(jnp.int32)


def touch_ends(entries, key, smallest, largest):
    dims = entries.shape
    place = [jax.random.randint(jax.random.fold_in(key, axis), (), 0, dims[axis]) for axis in range(len(dims))]
    entries = entries.at[tuple(place)].set(smallest)
    longest = dims.index(max(dims))
    place[longest] = (place[longest] + 1) % dims[longest]
    return entries.at[tuple(place)].set(largest)


def steps_of(rng, extent, pieces, smallest, high):
    gain = 1.0
    for axis_at, blocks in pieces:
        draws = jax.random.uniform(jax.random.fold_in(jax.random.fold_in(rng, 6), axis_at), (blocks,), jnp.float32, smallest / len(pieces), high / len(pieces))
        gain = gain * jnp.repeat(jnp.exp(draws), extent[axis_at] // blocks).reshape((-1,) + (1,) * (len(extent) - 1 - axis_at))
    return gain


def gaussian(key, extent, width, most, shards=(), kind=jnp.bfloat16):
    level = steps_of(key, extent, shards, -0.22, 0.18) if shards else 1.0
    values = jax.random.normal(key, extent, jnp.float32) * width * level
    return jnp.minimum(jnp.maximum(values, -most), most).astype(kind)


def setup_inputs(seed: int = 0, part: int = 0) -> dict:
    arg_keys = jax.random.split(jax.random.key(seed), 11)
    part_splits = jax.random.split(jax.random.fold_in(arg_keys[10], part), 11)
    return {
        "latent_query": draw_latent_query(jax.random.fold_in(jax.random.fold_in(arg_keys[10], part), 71), part),
        "latent_key": draw_latent_key(jax.random.fold_in(jax.random.fold_in(arg_keys[10], part), 71), part),
        "latent_value": gaussian(part_splits[2], (TILE_T, GRID_H, GRID_W, HEADS * HEAD_DIM), 1.0, 6.0, ((1, 4), (2, 4))),
        "latent_grad": gaussian(part_splits[3], (TILE_T, GRID_H, GRID_W, HEADS * HEAD_DIM), 1.0, 6.0, ((1, 4), (2, 4))),
        "text_query": draw_text_query(jax.random.fold_in(jax.random.fold_in(arg_keys[10], part), 71), part),
        "text_key": draw_text_key(jax.random.fold_in(jax.random.fold_in(arg_keys[10], part), 71), part),
        "text_value": gaussian(part_splits[6], (TEXT, HEADS * HEAD_DIM), 1.0, 6.0),
        "text_grad": gaussian(part_splits[7], (TEXT, HEADS * HEAD_DIM), 1.0, 6.0),
        "text_valid": touch_ends((jax.random.randint(part_splits[8], (TEXT,), 0, 4) < 3).astype(jnp.int32), jax.random.fold_in(part_splits[8], 1), 0, 1),
        "windows": draw_windows(jax.random.fold_in(arg_keys[10], 71), part),
    }


NEG_FILL = -1e30
exact_mode = lax.Precision.HIGHEST


def kept_bf16(value):
    return lax.optimization_barrier(value.astype(jnp.bfloat16)).astype(jnp.float32)


def contract(form, left, right):
    return jnp.einsum(form, left, right, precision=exact_mode)


def heads_of(array):
    return array.astype(jnp.float32).reshape(-1, HEADS, HEAD_DIM)


def reference(latent_query, latent_key, latent_value, latent_grad, text_query, text_key, text_value, text_grad, text_valid, windows):
    channels = HEADS * HEAD_DIM
    scale = HEAD_DIM ** -0.5
    tile_cols = GRID_W // TILE_W
    text_mask = text_valid == 1
    text_queries = heads_of(text_query)
    text_keys = heads_of(text_key)
    text_values = heads_of(text_value)
    text_grads = heads_of(text_grad)
    padding = ((0, 0), (TILE_H, TILE_H), (TILE_W, TILE_W), (0, 0))
    key_pad = jnp.pad(latent_key.astype(jnp.float32), padding)
    value_pad = jnp.pad(latent_value.astype(jnp.float32), padding)
    query_full = latent_query.astype(jnp.float32)
    grad_full = latent_grad.astype(jnp.float32)
    rows = jnp.arange(3 * TILE_H, dtype=jnp.int32) // TILE_H
    cols = jnp.arange(3 * TILE_W, dtype=jnp.int32) // TILE_W
    slots = 3 * rows[:, None] + cols[None, :]
    region_shape = (TILE_T, 3 * TILE_H, 3 * TILE_W, channels)
    block_shape = (TILE_T, TILE_H, TILE_W, channels)

    def tile_step(carry, tile):
        key_acc, value_acc, text_key_acc, text_value_acc = carry
        row_at = (tile // tile_cols) * TILE_H
        col_at = (tile % tile_cols) * TILE_W
        start = (jnp.int32(0), row_at.astype(jnp.int32), col_at.astype(jnp.int32), jnp.int32(0))
        queries = heads_of(lax.dynamic_slice(query_full, start, block_shape))
        grads = heads_of(lax.dynamic_slice(grad_full, start, block_shape))
        keys_near = heads_of(lax.dynamic_slice(key_pad, start, region_shape))
        values_near = heads_of(lax.dynamic_slice(value_pad, start, region_shape))
        keep = lax.dynamic_slice_in_dim(windows, tile, 1, 0)[0] >= 0
        plane = keep[slots]
        near_mask = jnp.broadcast_to(plane[None], (TILE_T, 3 * TILE_H, 3 * TILE_W)).reshape(-1)
        score_near = jnp.where(near_mask[None, None, :], contract("qhd,khd->hqk", queries, keys_near) * scale, NEG_FILL)
        score_text = jnp.where(text_mask[None, None, :], contract("qhd,khd->hqk", queries, text_keys) * scale, NEG_FILL)
        top = jnp.maximum(jnp.max(score_near, axis=-1), jnp.max(score_text, axis=-1))
        shift = kept_bf16(top)
        weight_near = jnp.exp(score_near - shift[..., None])
        weight_text = jnp.exp(score_text - shift[..., None])
        inverse = kept_bf16(1.0 / (jnp.sum(weight_near, axis=-1) + jnp.sum(weight_text, axis=-1)))
        prob_near = weight_near * inverse[..., None]
        prob_text = weight_text * inverse[..., None]
        low_near = kept_bf16(prob_near)
        low_text = kept_bf16(prob_text)
        attended = (contract("hqk,khd->qhd", low_near, values_near) + contract("hqk,khd->qhd", low_text, text_values)).astype(jnp.bfloat16)
        delta = kept_bf16(jnp.sum(grads * attended.astype(jnp.float32), axis=-1)).T
        dscore_near = kept_bf16(prob_near * (contract("qhd,khd->hqk", grads, values_near) - delta[..., None]))
        dscore_text = kept_bf16(prob_text * (contract("qhd,khd->hqk", grads, text_values) - delta[..., None]))
        query_grad = ((contract("hqk,khd->qhd", dscore_near, keys_near) + contract("hqk,khd->qhd", dscore_text, text_keys)) * scale).astype(jnp.bfloat16)
        key_add = contract("hqk,qhd->khd", dscore_near, queries).reshape(region_shape)
        value_add = contract("hqk,qhd->khd", low_near, grads).reshape(region_shape)
        key_acc = lax.dynamic_update_slice(key_acc, lax.dynamic_slice(key_acc, start, region_shape) + key_add, start)
        value_acc = lax.dynamic_update_slice(value_acc, lax.dynamic_slice(value_acc, start, region_shape) + value_add, start)
        text_key_acc = text_key_acc + contract("hqk,qhd->khd", dscore_text, queries)
        text_value_acc = text_value_acc + contract("hqk,qhd->khd", low_text, grads)
        return (key_acc, value_acc, text_key_acc, text_value_acc), (attended.reshape(block_shape), query_grad.reshape(block_shape))

    start_carry = (jnp.zeros_like(key_pad), jnp.zeros_like(value_pad), jnp.zeros((TEXT, HEADS, HEAD_DIM), jnp.float32), jnp.zeros((TEXT, HEADS, HEAD_DIM), jnp.float32))
    carry, stacked = lax.scan(tile_step, start_carry, jnp.arange(TILES, dtype=jnp.int32))
    key_acc, value_acc, text_key_acc, text_value_acc = carry

    def untile(blocks):
        grid = blocks.reshape(GRID_H // TILE_H, tile_cols, TILE_T, TILE_H, TILE_W, channels)
        return grid.transpose(2, 0, 3, 1, 4, 5).reshape(TILE_T, GRID_H, GRID_W, channels)

    latent_out = untile(stacked[0])
    grad_query = untile(stacked[1])

    keys_all = heads_of(latent_key)
    values_all = heads_of(latent_value)
    score_lat = contract("qhd,khd->hqk", text_queries, keys_all) * scale
    score_txt = jnp.where(text_mask[None, None, :], contract("qhd,khd->hqk", text_queries, text_keys) * scale, NEG_FILL)
    top = jnp.maximum(jnp.max(score_lat, axis=-1), jnp.max(score_txt, axis=-1))
    weight_lat = jnp.exp(score_lat - top[..., None])
    weight_txt = jnp.where(text_mask[None, None, :], jnp.exp(score_txt - top[..., None]), 0.0)
    total = jnp.sum(weight_lat, axis=-1) + jnp.sum(weight_txt, axis=-1)
    summed = contract("hqk,khd->qhd", weight_lat, values_all) + contract("hqk,khd->qhd", weight_txt, text_values)
    text_attended = (summed / total.T[..., None]).astype(jnp.bfloat16)
    lse = top + jnp.log(total)
    prob_lat = jnp.exp(score_lat - lse[..., None])
    prob_txt = jnp.where(text_mask[None, None, :], jnp.exp(score_txt - lse[..., None]), 0.0)
    text_delta = jnp.sum(text_grads * text_attended.astype(jnp.float32), axis=-1).T
    dscore_lat = kept_bf16(prob_lat * (contract("qhd,khd->hqk", text_grads, values_all) - text_delta[..., None]))
    dscore_txt = kept_bf16(prob_txt * (contract("qhd,khd->hqk", text_grads, text_values) - text_delta[..., None]))
    low_lat = kept_bf16(prob_lat)
    low_txt = kept_bf16(prob_txt)
    text_grad_query = ((contract("hqk,khd->qhd", dscore_lat, keys_all) + contract("hqk,khd->qhd", dscore_txt, text_keys)) * scale).astype(jnp.bfloat16).reshape(TEXT, channels)
    key_extra = contract("hqk,qhd->khd", dscore_lat, text_queries).reshape(TILE_T, GRID_H, GRID_W, channels)
    value_extra = contract("hqk,qhd->khd", low_lat, text_grads).reshape(TILE_T, GRID_H, GRID_W, channels)
    text_key_acc = text_key_acc + contract("hqk,qhd->khd", dscore_txt, text_queries)
    text_value_acc = text_value_acc + contract("hqk,qhd->khd", low_txt, text_grads)
    key_inner = key_acc[:, TILE_H:TILE_H + GRID_H, TILE_W:TILE_W + GRID_W]
    value_inner = value_acc[:, TILE_H:TILE_H + GRID_H, TILE_W:TILE_W + GRID_W]
    grad_key = ((key_inner + key_extra) * scale).astype(jnp.bfloat16)
    grad_value = (value_inner + value_extra).astype(jnp.bfloat16)
    text_out = text_attended.reshape(TEXT, channels)
    text_grad_key = (text_key_acc * scale).astype(jnp.bfloat16).reshape(TEXT, channels)
    text_grad_value = text_value_acc.astype(jnp.bfloat16).reshape(TEXT, channels)
    return (latent_out, grad_query, grad_key, grad_value, text_out, text_grad_query, text_grad_key, text_grad_value)
```

```python
import functools

import jax
import jax.numpy as jnp
from jax import lax
from jax.experimental import pallas as pl
from jax.experimental.pallas import tpu as pltpu
from jax.sharding import PartitionSpec as P

D = 128
SCALE = D ** (-0.5)
NEG = -1e30
F32 = jnp.float32
BF16 = jnp.bfloat16
PARAMS = pltpu.CompilerParams(
    dimension_semantics=("arbitrary",), vmem_limit_bytes=48 * 1024 * 1024
)


def dot_nt(a, b):
    return lax.dot_general(a, b, (((1,), (1,)), ((), ())), preferred_element_type=F32)


def dot_nn(a, b):
    return lax.dot_general(a, b, (((1,), (0,)), ((), ())), preferred_element_type=F32)


def dot_tn(a, b):
    return lax.dot_general(a, b, (((0,), (0,)), ((), ())), preferred_element_type=F32)


def round_bf16(x):
    return x.astype(BF16).astype(F32)


def pack_kernel(par, *refs):
    count = (len(refs) - 2) // 2
    kept, sent = refs[-2:]
    for at in range(count):
        kept[at] = refs[2 * at][...]
        sent[at] = refs[2 * at + 1][...]


def pack_halves(par, arrays):
    rows, channels = arrays[0].shape
    half = channels // 2
    count = len(arrays)
    specs = []
    for _ in arrays:
        specs.append(pl.BlockSpec((rows, half), lambda i, p: (0, p[0])))
        specs.append(pl.BlockSpec((rows, half), lambda i, p: (0, 1 - p[0])))
    out = jax.ShapeDtypeStruct((count, rows, half), BF16)
    return pl.pallas_call(
        pack_kernel,
        grid_spec=pltpu.PrefetchScalarGridSpec(
            num_scalar_prefetch=1,
            grid=(1,),
            in_specs=specs,
            out_specs=[pl.BlockSpec((count, rows, half), lambda i, p: (0, 0, 0))] * 2,
        ),
        out_shape=[out, out],
        compiler_params=PARAMS,
        name="pack_halves",
    )(par, *[a for a in arrays for _ in range(2)])


def text_scores(kv, tq, tg, tk, tv, bias):
    query, grad = tq[...], tg[...]
    near = dot_nt(kv[0], query) * SCALE
    own = dot_nt(tk[...], query) * SCALE + bias[...]
    return near, own, dot_nt(kv[1], grad), dot_nt(tv[...], grad)


def text_stats_kernel(par, kv, tq, tg, tk, tv, bias, stats):
    near, own, dp_near, dp_own = text_scores(kv, tq, tg, tk, tv, bias)
    top = jnp.maximum(
        jnp.max(near, axis=0, keepdims=True), jnp.max(own, axis=0, keepdims=True)
    )
    e_near = jnp.exp(near - top)
    e_own = jnp.exp(own - top)
    total = jnp.sum(e_near, axis=0, keepdims=True) + jnp.sum(e_own, axis=0, keepdims=True)
    mix = jnp.sum(e_near * dp_near, axis=0, keepdims=True) + jnp.sum(
        e_own * dp_own, axis=0, keepdims=True
    )
    stats[0] = jnp.concatenate([top, total, mix, jnp.zeros((5, top.shape[1]), F32)], axis=0)


def text_grads_kernel(par, gathered, kv, tq, tg, tk, tv, bias, rows, self_keys, near_keys):
    near, own, dp_near, dp_own = text_scores(kv, tq, tg, tk, tv, bias)
    parts = gathered[:, 0, 0]
    tops = parts[:, 0, :]
    top = jnp.max(tops, axis=0, keepdims=True)
    factor = jnp.exp(tops - top)
    total = jnp.sum(parts[:, 1, :] * factor, axis=0, keepdims=True)
    delta = jnp.sum(parts[:, 2, :] * factor, axis=0, keepdims=True) / total
    lse = top + jnp.log(total)
    p_near = jnp.exp(near - lse)
    p_own = jnp.exp(own - lse)
    low_near = p_near.astype(BF16)
    low_own = p_own.astype(BF16)
    ds_near = (p_near * (dp_near - delta)).astype(BF16)
    ds_own = (p_own * (dp_own - delta)).astype(BF16)
    query, grad = tq[...], tg[...]
    rows[0] = (dot_tn(low_near, kv[1]) + dot_tn(low_own, tv[...])).astype(BF16)
    rows[1] = (dot_tn(ds_near, kv[0]) + dot_tn(ds_own, tk[...])).astype(BF16)
    self_keys[0] = dot_nn(ds_own, query)
    self_keys[1] = dot_nn(low_own, grad)
    near_keys[0] = dot_nn(ds_near, query)
    near_keys[1] = dot_nn(low_near, grad)


def query_kernel(count, par, gates, qg, *refs):
    tiles = refs[:count]
    tk, tv, bias, self_keys, kept, sent, stats, text_rows, score = refs[count:]
    half = qg.shape[1] // 2
    query, grad = qg[0], qg[1]
    size = qg.shape[1]
    text = tk.shape[0]
    top = None
    for at in range(count):
        part = dot_nt(tiles[at][0], query) * SCALE + gates[at]
        score[at * size : (at + 1) * size] = part
        peak = jnp.max(part, axis=0, keepdims=True)
        top = peak if top is None else jnp.maximum(top, peak)
    part = dot_nt(tk[...], query) * SCALE + bias[...][:, :1]
    score[count * size : count * size + text] = part
    shift = round_bf16(jnp.maximum(top, jnp.max(part, axis=0, keepdims=True)))
    spans = [(at * size, size) for at in range(count)] + [(count * size, text)]
    total = jnp.zeros_like(shift)
    for first, length in spans:
        weight = jnp.exp(score[first : first + length] - shift)
        score[first : first + length] = weight
        total = total + jnp.sum(weight, axis=0, keepdims=True)
    inverse = round_bf16(1.0 / total)
    keys = [(lambda at=at: tiles[at][0]) for at in range(count)] + [lambda: tk[...]]
    values = [(lambda at=at: tiles[at][1]) for at in range(count)] + [lambda: tv[...]]
    out = jnp.zeros((D, size), F32)
    for at, (first, length) in enumerate(spans):
        low = (score[first : first + length] * inverse).astype(BF16)
        out = out + dot_tn(values[at](), low)
        if at == count:
            text_rows[1] = (self_keys[1] + dot_nn(low, grad)).astype(BF16)
    out = round_bf16(out)
    grad_t = grad.astype(F32).T
    delta = round_bf16(jnp.sum(grad_t * out, axis=0, keepdims=True))
    query_grad = jnp.zeros((D, size), F32)
    for at, (first, length) in enumerate(spans):
        dp = dot_nt(values[at](), grad)
        ds = (score[first : first + length] * inverse * (dp - delta)).astype(BF16)
        query_grad = query_grad + dot_tn(keys[at](), ds)
        if at == count:
            text_rows[0] = (self_keys[0] + dot_nn(ds, query)).astype(BF16)
    out = out.T.astype(BF16)
    query_grad = (query_grad * SCALE).T.astype(BF16)
    kept[0] = out[:half]
    kept[1] = query_grad[:half]
    sent[0] = out[half:]
    sent[1] = query_grad[half:]
    stats[0] = jnp.concatenate([shift, inverse, delta, jnp.zeros((5, size), F32)], axis=0)


def key_kernel(count, gates, kv, near_keys, *refs):
    tiles = refs[:count]
    stats = refs[count : 2 * count]
    kept, sent = refs[2 * count :]
    half = kv.shape[1] // 2
    key, value = kv[0], kv[1]
    key_grad = near_keys[0]
    value_grad = near_keys[1]
    for at in range(count):
        query, grad = tiles[at][0], tiles[at][1]
        shift, inverse, delta = (stats[at][0, row : row + 1, :] for row in range(3))
        prob = jnp.exp(dot_nt(key, query) * SCALE + (gates[at] - shift)) * inverse
        ds = (prob * (dot_nt(value, grad) - delta)).astype(BF16)
        value_grad = value_grad + dot_nn(prob.astype(BF16), grad)
        key_grad = key_grad + dot_nn(ds, query)
    key_grad = (key_grad * SCALE).astype(BF16)
    value_grad = value_grad.astype(BF16)
    kept[0] = key_grad[:half]
    kept[1] = value_grad[:half]
    sent[0] = key_grad[half:]
    sent[1] = value_grad[half:]


def shifted(value, axis, steps):
    count = lax.axis_size(axis)
    pairs = [(at, at + steps) for at in range(count) if 0 <= at + steps < count]
    return lax.ppermute(value, axis, pairs)


def swapped(value, stride):
    count = lax.axis_size("hgt")
    return lax.ppermute(value, "hgt", [(at, at ^ stride) for at in range(count)])


def fetch(value):
    if lax.axis_size("hgt") == 4:
        columns = [value, swapped(value, 2)]
    else:
        columns = [value, shifted(value, "hgt", 2), shifted(value, "hgt", -2)]
    return [
        part
        for column in columns
        for part in (column, shifted(column, "wid", 1), shifted(column, "wid", -1))
    ]


def halves_back(parity, mine, theirs):
    return jnp.where(
        parity == 0,
        jnp.concatenate([mine, theirs], axis=-1),
        jnp.concatenate([theirs, mine], axis=-1),
    )


def per_device(
    latent_query,
    latent_key,
    latent_value,
    latent_grad,
    text_query,
    text_key,
    text_value,
    text_grad,
    text_valid,
    windows,
):
    block = latent_query.shape
    channels = block[3]
    rows = block[0] * block[1] * block[2]
    size = 2 * rows
    width = channels // 2
    heads = width // D
    text = text_query.shape[0]
    wid_size, hgt_size = lax.axis_size("wid"), lax.axis_size("hgt")
    devices = wid_size * hgt_size
    wid_at, hgt_at = lax.axis_index("wid"), lax.axis_index("hgt")
    parity = hgt_at % 2
    tile_row, tile_rows = hgt_at // 2, hgt_size // 2
    tile_here = tile_row * wid_size + wid_at
    par = parity.astype(jnp.int32).reshape(1)

    row_steps = [0, 1 - 2 * tile_row] if hgt_size == 4 else [0, -1, 1]
    sees, seen = [], []
    for dr in row_steps:
        for dc in (0, -1, 1):
            row, col = tile_row + dr, wid_at + dc
            inside = (row >= 0) & (row < tile_rows) & (col >= 0) & (col < wid_size)
            other = jnp.clip(row, 0, tile_rows - 1) * wid_size + jnp.clip(col, 0, wid_size - 1)
            slot = (dr + 1) * 3 + dc + 1
            sees.append(inside & (windows[tile_here, slot] >= 0))
            seen.append(inside & (windows[other, 8 - slot] >= 0))
    count = len(sees)
    gate_query = jnp.where(jnp.stack(sees), 0.0, NEG).astype(F32)
    gate_key = jnp.where(jnp.stack(seen), 0.0, NEG).astype(F32)
    text_bias = jnp.broadcast_to(jnp.where(text_valid == 1, 0.0, NEG).astype(F32)[:, None], (text, text))
    self_bias = jnp.where(tile_here == 0, text_bias, NEG)

    flat = [a.reshape(rows, channels) for a in (latent_key, latent_value, latent_query, latent_grad)]
    kv_kept, kv_sent = pack_halves(par, flat[:2])
    qg_kept, qg_sent = pack_halves(par, flat[2:])
    kv = jnp.concatenate([kv_kept, swapped(kv_sent, 1)], axis=1)
    qg = jnp.concatenate([qg_kept, swapped(qg_sent, 1)], axis=1)
    kv_tiles = fetch(kv)
    qg_tiles = fetch(qg)

    tile_spec = pl.BlockSpec((2, size, D), lambda h, *_: (0, 0, h))
    text_spec = pl.BlockSpec((text, D), lambda h, p, *_: (0, p[0] * heads + h))
    bias_spec = pl.BlockSpec((text, text), lambda h, *_: (0, 0))
    row_spec = pl.BlockSpec((2, text, D), lambda h, *_: (0, 0, h))
    half_spec = pl.BlockSpec((2, rows, D), lambda h, *_: (0, 0, h))
    stat_spec = pl.BlockSpec((1, 8, size), lambda h, *_: (h, 0, 0))
    smem = pl.BlockSpec(memory_space=pltpu.SMEM)

    text_stats = pl.pallas_call(
        text_stats_kernel,
        grid_spec=pltpu.PrefetchScalarGridSpec(
            num_scalar_prefetch=1,
            grid=(heads,),
            in_specs=[tile_spec] + [text_spec] * 4 + [bias_spec],
            out_specs=pl.BlockSpec((1, 8, text), lambda h, p: (h, 0, 0)),
        ),
        out_shape=jax.ShapeDtypeStruct((heads, 8, text), F32),
        compiler_params=PARAMS,
        cost_estimate=pl.CostEstimate(
            flops=4 * heads * (size + text) * text * D, bytes_accessed=4 * size * width, transcendentals=0
        ),
        name="text_stats",
    )(par, kv, text_query, text_grad, text_key, text_value, self_bias)
    gathered = lax.all_gather(text_stats, ("wid", "hgt")).reshape(devices // 2, 2, heads, 8, text)

    text_rows, self_keys, near_keys = pl.pallas_call(
        text_grads_kernel,
        grid_spec=pltpu.PrefetchScalarGridSpec(
            num_scalar_prefetch=1,
            grid=(heads,),
            in_specs=[
                pl.BlockSpec((devices // 2, 1, 1, 8, text), lambda h, p: (0, p[0], h, 0, 0)),
                tile_spec,
            ]
            + [text_spec] * 4
            + [bias_spec],
            out_specs=[row_spec, row_spec, tile_spec],
        ),
        out_shape=[
            jax.ShapeDtypeStruct((2, text, width), BF16),
            jax.ShapeDtypeStruct((2, text, width), F32),
            jax.ShapeDtypeStruct((2, size, width), F32),
        ],
        compiler_params=PARAMS,
        cost_estimate=pl.CostEstimate(
            flops=12 * heads * (size + text) * text * D, bytes_accessed=8 * size * width, transcendentals=0
        ),
        name="text_grads",
    )(par, gathered, kv, text_query, text_grad, text_key, text_value, self_bias)

    work = heads * size * (count * size + text) * D
    half_shape = jax.ShapeDtypeStruct((2, rows, width), BF16)
    query_kept, query_sent, stats, key_rows = pl.pallas_call(
        functools.partial(query_kernel, count),
        grid_spec=pltpu.PrefetchScalarGridSpec(
            num_scalar_prefetch=1,
            grid=(heads,),
            in_specs=[smem, tile_spec]
            + [tile_spec] * count
            + [text_spec, text_spec, bias_spec, row_spec],
            out_specs=[half_spec, half_spec, stat_spec, row_spec],
            scratch_shapes=[pltpu.VMEM((count * size + text, size), F32)],
        ),
        out_shape=[
            half_shape,
            half_shape,
            jax.ShapeDtypeStruct((heads, 8, size), F32),
            jax.ShapeDtypeStruct((2, text, width), BF16),
        ],
        compiler_params=PARAMS,
        cost_estimate=pl.CostEstimate(
            flops=8 * work, bytes_accessed=4 * size * width * (count + 2), transcendentals=work // D
        ),
        name="query_side",
    )(par, gate_query, qg, *kv_tiles, text_key, text_value, text_bias, self_keys)

    stat_tiles = fetch(stats)
    query_back = swapped(query_sent, 1)
    packed = jnp.concatenate([text_rows, key_rows], axis=0)
    owned = text // devices
    packed = packed.reshape(4, devices, owned, width)
    landed = lax.all_to_all(packed, ("wid", "hgt"), 1, 1)

    key_kept, key_sent = pl.pallas_call(
        functools.partial(key_kernel, count),
        grid_spec=pltpu.PrefetchScalarGridSpec(
            num_scalar_prefetch=1,
            grid=(heads,),
            in_specs=[tile_spec, tile_spec] + [tile_spec] * count + [stat_spec] * count,
            out_specs=[half_spec, half_spec],
        ),
        out_shape=[half_shape, half_shape],
        compiler_params=PARAMS,
        cost_estimate=pl.CostEstimate(
            flops=8 * work, bytes_accessed=4 * size * width * (count + 2), transcendentals=work // D
        ),
        name="key_side",
    )(gate_key, kv, near_keys, *qg_tiles, *stat_tiles)
    key_back = swapped(key_sent, 1)

    latent = [
        halves_back(parity, mine[at], theirs[at]).reshape(block)
        for mine, theirs in ((query_kept, query_back), (key_kept, key_back))
        for at in range(2)
    ]
    summed = jnp.sum(landed.reshape(4, devices // 2, 2, owned, width).astype(F32), axis=1)
    summed = jnp.swapaxes(summed, 1, 2).reshape(4, owned, channels)
    text_outs = [
        summed[0].astype(BF16),
        (summed[1] * SCALE).astype(BF16),
        (summed[2] * SCALE).astype(BF16),
        summed[3].astype(BF16),
    ]
    return tuple(latent + text_outs)


def solution(mesh):
    tiles = P("grp", "hgt", "wid", None)
    rows = P(("grp", "wid", "hgt"), None)
    return jax.shard_map(
        per_device,
        mesh=mesh,
        in_specs=(tiles,) * 4 + (P("grp", None),) * 4 + (P("grp"), P()),
        out_specs=(tiles,) * 4 + (rows,) * 4,
        check_vma=False,
    )
```

```python
import functools

import jax
import jax.numpy as jnp
from jax import lax
from jax.experimental import pallas as pl
from jax.experimental.pallas import tpu as pltpu
from jax.sharding import PartitionSpec as P

D = 128
SCALE = D ** (-0.5)
NEG = -1e30
F32 = jnp.float32
BF16 = jnp.bfloat16
def dot_nt(a, b):
    return lax.dot_general(a, b, (((1,), (1,)), ((), ())), preferred_element_type=F32)


def dot_nn(a, b):
    return lax.dot_general(a, b, (((1,), (0,)), ((), ())), preferred_element_type=F32)


def dot_tn(a, b):
    return lax.dot_general(a, b, (((0,), (0,)), ((), ())), preferred_element_type=F32)


def round_bf16(x):
    return x.astype(BF16).astype(F32)


def when(conds, run):
    conds = [c for c in conds if c is not None]
    if not conds:
        run()
        return
    total = conds[0]
    for c in conds[1:]:
        total = jnp.logical_and(total, c)
    pl.when(total)(run)


def neither(conds, run):
    conds = [c for c in conds if c is not None]
    if conds:
        total = conds[0]
        for c in conds[1:]:
            total = jnp.logical_and(total, c)
        pl.when(jnp.logical_not(total))(run)


def whole_kernel(
    wid_size,
    hgt_size,
    gate_query,
    gate_key,
    latent_key,
    latent_value,
    latent_query,
    latent_grad,
    text_query,
    text_key,
    text_value,
    text_grad,
    text_bias,
    self_bias,
    out0,
    out1,
    out2,
    out3,
    text_out,
    tiles,
    score,
    stats,
    text_stats,
    near_keys,
    self_keys,
    text_parts,
    text_landed,
    back,
    landed,
    load_sem,
    half_send,
    half_recv,
    tile_send,
    tile_recv,
    stat_send,
    stat_recv,
    text_send,
    text_recv,
    part_send,
    part_recv,
    back_send,
    back_recv,
):
    outs = (out0, out1, out2, out3)
    count = tiles.shape[1]
    size, width = tiles.shape[2], tiles.shape[3]
    half = size // 2
    heads = width // D
    text = text_query.shape[0]
    devices = wid_size * hgt_size
    tile_rows = hgt_size // 2
    tile_count = devices // 2
    grain = text_parts.shape[2]
    owned = text // devices

    wid, hgt = lax.axis_index("wid"), lax.axis_index("hgt")
    par = lax.rem(hgt, 2)
    row = hgt // 2
    rank = wid * hgt_size + hgt
    mine = pl.multiple_of(par * width, D)
    other = pl.multiple_of((1 - par) * width, D)
    tile_at = row * wid_size + wid
    mate = {"wid": wid, "hgt": hgt + 1 - 2 * par}

    def rank_peer(step):
        peer = lax.rem(rank + step, devices)
        return peer, {"wid": peer // hgt_size, "hgt": lax.rem(peer, hgt_size)}

    def tile_peer(step):
        peer = lax.rem(tile_at + step, tile_count)
        return {"wid": lax.rem(peer, wid_size), "hgt": 2 * (peer // wid_size) + par}

    def copy(src, dst, send, recv, device):
        return pltpu.make_async_remote_copy(
            src_ref=src,
            dst_ref=dst,
            send_sem=send,
            recv_sem=recv,
            device_id=device,
            device_id_type=pl.DeviceIdType.MESH,
        )

    has_left, has_right = wid > 0, wid < wid_size - 1
    left = {"wid": jnp.maximum(wid - 1, 0), "hgt": hgt}
    right = {"wid": jnp.minimum(wid + 1, wid_size - 1), "hgt": hgt}
    sides = [(1, right, has_right, has_left), (2, left, has_left, has_right)]
    if hgt_size == 4:
        uprights = [(1, {"wid": wid, "hgt": lax.rem(hgt + 2, 4)}, None, None)]
    else:
        has_up, has_down = row > 0, row < tile_rows - 1
        down = {"wid": wid, "hgt": jnp.minimum(hgt + 2, hgt_size - 2 + par)}
        up = {"wid": wid, "hgt": jnp.maximum(hgt - 2, par)}
        uprights = [(1, down, has_down, has_up), (2, up, has_up, has_down)]

    barrier = pltpu.get_barrier_semaphore()

    @pl.loop(1, devices)
    def _(step):
        _, device = rank_peer(step)
        pl.semaphore_signal(barrier, inc=1, device_id=device, device_id_type=pl.DeviceIdType.MESH)

    arrays = (latent_key, latent_value, latent_query, latent_grad)
    loads = [
        pltpu.make_async_copy(
            arrays[a].at[:, pl.ds(mine, width)], tiles.at[a, 0, pl.ds(0, half)], load_sem.at[a]
        )
        for a in range(4)
    ]
    for load in loads:
        load.start()
    pl.semaphore_wait(barrier, devices - 1)
    halves = [
        copy(
            arrays[a].at[:, pl.ds(other, width)],
            tiles.at[a, 0, pl.ds(half, half)],
            half_send.at[a],
            half_recv.at[a],
            mate,
        )
        for a in range(4)
    ]
    for move in halves:
        move.start()

    def hop(a, source, target, device):
        return copy(
            tiles.at[a, source],
            tiles.at[a, target],
            tile_send.at[a, target],
            tile_recv.at[a, target],
            device,
        )

    def stat_hop(source, target, device):
        return copy(
            stats.at[source],
            stats.at[target],
            stat_send.at[target],
            stat_recv.at[target],
            device,
        )

    sent = []

    def launch(make, conds):
        when(conds, lambda: make().start())
        sent.append((make, conds))

    def arrive(make, conds):
        when(conds, lambda: make().wait_recv())

    def first_hops(a):
        for r, device, go, _ in uprights:
            launch(functools.partial(hop, a, 0, 3 * r, device), [go])
        for c, device, go, _ in sides:
            launch(functools.partial(hop, a, 0, c, device), [go])

    def second_hops(a):
        if a != 2:
            for r, device, _, come in uprights:
                arrive(lambda: hop(a, 0, 3 * r, device), [come])
            for r, _, _, come in uprights:
                for c, device, go, _ in sides:
                    launch(functools.partial(hop, a, 3 * r, 3 * r + c, device), [go, come])
        else:
            for c, device, _, come in sides:
                arrive(lambda: hop(a, 0, c, device), [come])
            for r, device, go, _ in uprights:
                for c, _, _, come in sides:
                    launch(functools.partial(hop, a, c, 3 * r + c, device), [go, come])

    def all_arrived(a):
        if a != 2:
            for c, device, _, come in sides:
                arrive(lambda: hop(a, 0, c, device), [come])
        else:
            for r, device, _, come in uprights:
                arrive(lambda: hop(a, 0, 3 * r, device), [come])
        for r, _, _, come_row in uprights:
            for c, device, _, come in sides:
                arrive(lambda: hop(a, 0, 3 * r + c, device), [come, come_row])

    def clear(slot, conds):
        def run():
            for a in range(4):
                tiles[a, slot] = jnp.zeros((size, width), BF16)
            stats[slot] = jnp.zeros(stats.shape[1:], F32)

        neither(conds, run)

    for a in range(4):
        loads[a].wait()
        halves[a].wait_recv()
        first_hops(a)
    for c, _, _, come in sides:
        clear(c, [come])
    for r, _, _, come_row in uprights:
        clear(3 * r, [come_row])
        for c, _, _, come in sides:
            clear(3 * r + c, [come, come_row])

    def lanes(h):
        return pl.ds(pl.multiple_of(h * D, D), D)

    def text_lanes(h):
        return pl.ds(pl.multiple_of(mine + h * D, D), D)

    def text_scores(h):
        query, grad = text_query[:, text_lanes(h)], text_grad[:, text_lanes(h)]
        near = dot_nt(tiles[0, 0, :, lanes(h)], query) * SCALE
        own = dot_nt(text_key[:, text_lanes(h)], query) * SCALE + self_bias[...]
        dp_near = dot_nt(tiles[1, 0, :, lanes(h)], grad)
        dp_own = dot_nt(text_value[:, text_lanes(h)], grad)
        return query, grad, near, own, dp_near, dp_own

    @pl.loop(0, heads)
    def _(h):
        _, _, near, own, dp_near, dp_own = text_scores(h)
        top = jnp.maximum(
            jnp.max(near, axis=0, keepdims=True), jnp.max(own, axis=0, keepdims=True)
        )
        e_near = jnp.exp(near - top)
        e_own = jnp.exp(own - top)
        total = jnp.sum(e_near, axis=0, keepdims=True) + jnp.sum(e_own, axis=0, keepdims=True)
        mix = jnp.sum(e_near * dp_near, axis=0, keepdims=True) + jnp.sum(
            e_own * dp_own, axis=0, keepdims=True
        )
        text_stats[0, h] = jnp.concatenate(
            [top, total, mix, jnp.zeros((5, top.shape[1]), F32)], axis=0
        )

    def text_copy(step):
        return copy(
            text_stats.at[0],
            text_stats.at[step],
            text_send.at[step],
            text_recv.at[step],
            tile_peer(step),
        )

    @pl.loop(1, tile_count)
    def _(step):
        text_copy(step).start()

    second_hops(0)
    second_hops(1)

    @pl.loop(1, tile_count)
    def _(step):
        text_copy(step).wait_recv()

    def spread(at, h, value):
        text_parts[:, at, :, lanes(h)] = value.reshape(text // grain, grain, D).astype(BF16)

    @pl.loop(0, heads)
    def _(h):
        query, grad, near, own, dp_near, dp_own = text_scores(h)
        parts = text_stats[:, h]
        tops = parts[:, 0, :]
        top = jnp.max(tops, axis=0, keepdims=True)
        factor = jnp.exp(tops - top)
        total = jnp.sum(parts[:, 1, :] * factor, axis=0, keepdims=True)
        delta = jnp.sum(parts[:, 2, :] * factor, axis=0, keepdims=True) / total
        lse = top + jnp.log(total)
        p_near = jnp.exp(near - lse)
        p_own = jnp.exp(own - lse)
        low_near = p_near.astype(BF16)
        low_own = p_own.astype(BF16)
        ds_near = (p_near * (dp_near - delta)).astype(BF16)
        ds_own = (p_own * (dp_own - delta)).astype(BF16)
        spread(
            0,
            h,
            dot_tn(low_near, tiles[1, 0, :, lanes(h)])
            + dot_tn(low_own, text_value[:, text_lanes(h)]),
        )
        spread(
            1,
            h,
            dot_tn(ds_near, tiles[0, 0, :, lanes(h)]) + dot_tn(ds_own, text_key[:, text_lanes(h)]),
        )
        self_keys[0, :, lanes(h)] = dot_nn(ds_own, query)
        self_keys[1, :, lanes(h)] = dot_nn(low_own, grad)
        near_keys[0, :, lanes(h)] = dot_nn(ds_near, query)
        near_keys[1, :, lanes(h)] = dot_nn(low_near, grad)

    second_hops(2)
    second_hops(3)
    all_arrived(0)
    all_arrived(1)

    spans = [(at * size, size) for at in range(count)] + [(count * size, text)]

    @pl.loop(0, heads)
    def _(h):
        query, grad = tiles[2, 0, :, lanes(h)], tiles[3, 0, :, lanes(h)]

        def key_of(at):
            return tiles[0, at, :, lanes(h)] if at < count else text_key[:, text_lanes(h)]

        def value_of(at):
            return tiles[1, at, :, lanes(h)] if at < count else text_value[:, text_lanes(h)]

        top = None
        for at, (first, length) in enumerate(spans):
            part = dot_nt(key_of(at), query) * SCALE
            part = part + (gate_query[at] if at < count else text_bias[...][:, :1])
            score[first : first + length] = part
            peak = jnp.max(part, axis=0, keepdims=True)
            top = peak if top is None else jnp.maximum(top, peak)
        shift = round_bf16(top)
        total = jnp.zeros_like(shift)
        for first, length in spans:
            weight = jnp.exp(score[first : first + length] - shift)
            score[first : first + length] = weight
            total = total + jnp.sum(weight, axis=0, keepdims=True)
        inverse = round_bf16(1.0 / total)
        out = jnp.zeros((D, size), F32)
        for at, (first, length) in enumerate(spans):
            low = (score[first : first + length] * inverse).astype(BF16)
            out = out + dot_tn(value_of(at), low)
            if at == count:
                spread(3, h, self_keys[1, :, lanes(h)] + dot_nn(low, grad))
        out = round_bf16(out)
        delta = round_bf16(jnp.sum(grad.astype(F32).T * out, axis=0, keepdims=True))
        query_grad = jnp.zeros((D, size), F32)
        for at, (first, length) in enumerate(spans):
            dp = dot_nt(value_of(at), grad)
            ds = (score[first : first + length] * inverse * (dp - delta)).astype(BF16)
            query_grad = query_grad + dot_tn(key_of(at), ds)
            if at == count:
                spread(2, h, self_keys[0, :, lanes(h)] + dot_nn(ds, query))
        for at, value in enumerate((out.T, (query_grad * SCALE).T)):
            value = value.astype(BF16)
            outs[at][:, text_lanes(h)] = value[:half]
            back[at, :, lanes(h)] = value[half:]
        stats[0, h] = jnp.concatenate([shift, inverse, delta, jnp.zeros((5, size), F32)], axis=0)

    for r, device, go, _ in uprights:
        launch(functools.partial(stat_hop, 0, 3 * r, device), [go])
    for c, device, go, _ in sides:
        launch(functools.partial(stat_hop, 0, c, device), [go])

    def part_copy(step):
        peer, device = rank_peer(step)
        return copy(
            text_parts.at[peer * owned // grain],
            text_landed.at[step],
            part_send.at[step],
            part_recv.at[step],
            device,
        )

    @pl.loop(1, devices)
    def _(step):
        part_copy(step).start()

    def back_copy(at):
        return copy(back.at[at], landed.at[at], back_send.at[at], back_recv.at[at], mate)

    for at in range(2):
        back_copy(at).start()

    for r, device, _, come in uprights:
        arrive(lambda: stat_hop(0, 3 * r, device), [come])
    for r, _, _, come in uprights:
        for c, device, go, _ in sides:
            launch(functools.partial(stat_hop, 3 * r, 3 * r + c, device), [go, come])
    for c, device, _, come in sides:
        arrive(lambda: stat_hop(0, c, device), [come])
    for r, _, _, come_row in uprights:
        for c, device, _, come in sides:
            arrive(lambda: stat_hop(0, 3 * r + c, device), [come, come_row])
    all_arrived(2)
    all_arrived(3)

    @pl.loop(0, heads)
    def _(h):
        key, value = tiles[0, 0, :, lanes(h)], tiles[1, 0, :, lanes(h)]
        key_grad = near_keys[0, :, lanes(h)]
        value_grad = near_keys[1, :, lanes(h)]
        for at in range(count):
            query, grad = tiles[2, at, :, lanes(h)], tiles[3, at, :, lanes(h)]
            rows = stats[at, h]
            shift, inverse, delta = rows[0:1], rows[1:2], rows[2:3]
            prob = jnp.exp(dot_nt(key, query) * SCALE + (gate_key[at] - shift)) * inverse
            ds = (prob * (dot_nt(value, grad) - delta)).astype(BF16)
            value_grad = value_grad + dot_nn(prob.astype(BF16), grad)
            key_grad = key_grad + dot_nn(ds, query)
        for at, grads in ((2, key_grad * SCALE), (3, value_grad)):
            grads = grads.astype(BF16)
            outs[at][:, text_lanes(h)] = grads[:half]
            back[at, :, lanes(h)] = grads[half:]

    for at in range(2, 4):
        back_copy(at).start()

    @pl.loop(1, devices)
    def _(step):
        part_copy(step).wait_recv()

    own_part = text_parts[rank * owned // grain].astype(F32)

    def add_pair(step, sums):
        same = sums[0] + text_landed[2 * step].astype(F32)
        return same, sums[1] + text_landed[2 * step + 1].astype(F32)

    same, cross = lax.fori_loop(
        1, devices // 2, add_pair, (own_part, text_landed[1].astype(F32))
    )
    text_out[:, :, pl.ds(mine, width)] = same
    text_out[:, :, pl.ds(other, width)] = cross

    for at in range(4):
        back_copy(at).wait_recv()
        outs[at][:, pl.ds(other, width)] = landed[at]

    for move in halves:
        move.wait_send()
    for make, conds in sent:
        when(conds, lambda: make().wait_send())

    @pl.loop(1, tile_count)
    def _(step):
        text_copy(step).wait_send()

    @pl.loop(1, devices)
    def _(step):
        part_copy(step).wait_send()

    for at in range(4):
        back_copy(at).wait_send()


def per_device(
    latent_query,
    latent_key,
    latent_value,
    latent_grad,
    text_query,
    text_key,
    text_value,
    text_grad,
    text_valid,
    windows,
):
    block = latent_query.shape
    channels = block[3]
    rows = block[0] * block[1] * block[2]
    size = 2 * rows
    width = channels // 2
    heads = width // D
    text = text_query.shape[0]
    wid_size, hgt_size = lax.axis_size("wid"), lax.axis_size("hgt")
    devices = wid_size * hgt_size
    wid_at, hgt_at = lax.axis_index("wid"), lax.axis_index("hgt")
    tile_row, tile_rows = hgt_at // 2, hgt_size // 2
    tile_here = tile_row * wid_size + wid_at

    row_steps = [0, 1 - 2 * tile_row] if hgt_size == 4 else [0, -1, 1]
    sees, seen = [], []
    for dr in row_steps:
        for dc in (0, -1, 1):
            row, col = tile_row + dr, wid_at + dc
            inside = (row >= 0) & (row < tile_rows) & (col >= 0) & (col < wid_size)
            other = jnp.clip(row, 0, tile_rows - 1) * wid_size + jnp.clip(col, 0, wid_size - 1)
            slot = (dr + 1) * 3 + dc + 1
            sees.append(inside & (windows[tile_here, slot] >= 0))
            seen.append(inside & (windows[other, 8 - slot] >= 0))
    count = len(sees)
    gate_query = jnp.where(jnp.stack(sees), 0.0, NEG).astype(F32)
    gate_key = jnp.where(jnp.stack(seen), 0.0, NEG).astype(F32)
    text_bias = jnp.broadcast_to(
        jnp.where(text_valid == 1, 0.0, NEG).astype(F32)[:, None], (text, text)
    )
    self_bias = jnp.where(tile_here == 0, text_bias, NEG)

    owned = text // devices
    grain = max(owned, 8)
    flat = [a.reshape(rows, channels) for a in (latent_key, latent_value, latent_query, latent_grad)]
    smem = pl.BlockSpec(memory_space=pltpu.SMEM)
    hbm = pl.BlockSpec(memory_space=pl.ANY)
    vmem = pl.BlockSpec(memory_space=pltpu.VMEM)
    dma = pltpu.SemaphoreType.DMA
    results = pl.pallas_call(
        functools.partial(whole_kernel, wid_size, hgt_size),
        in_specs=[smem] * 2 + [hbm] * 4 + [vmem] * 6,
        out_specs=[vmem] * 5,
        out_shape=[jax.ShapeDtypeStruct((rows, channels), BF16)] * 4
        + [jax.ShapeDtypeStruct((4, grain, channels), F32)],
        scratch_shapes=[
            pltpu.VMEM((4, count, size, width), BF16),
            pltpu.VMEM((count * size + text, size), F32),
            pltpu.VMEM((count, heads, 8, size), F32),
            pltpu.VMEM((devices // 2, heads, 8, text), F32),
            pltpu.VMEM((2, size, width), F32),
            pltpu.VMEM((2, text, width), F32),
            pltpu.VMEM((text // grain, 4, grain, width), BF16),
            pltpu.VMEM((devices, 4, grain, width), BF16),
            pltpu.VMEM((4, rows, width), BF16),
            pltpu.VMEM((4, rows, width), BF16),
            dma((4,)),
            dma((4,)),
            dma((4,)),
            dma((4, count)),
            dma((4, count)),
            dma((count,)),
            dma((count,)),
            dma((devices // 2,)),
            dma((devices // 2,)),
            dma((devices,)),
            dma((devices,)),
            dma((4,)),
            dma((4,)),
        ],
        compiler_params=pltpu.CompilerParams(
            collective_id=0, has_side_effects=True, vmem_limit_bytes=52 * 1024 * 1024
        ),
        name="joint_attention",
    )(
        gate_query,
        gate_key,
        *flat,
        text_query,
        text_key,
        text_value,
        text_grad,
        text_bias,
        self_bias,
    )
    latent = [a.reshape(block) for a in results[:4]]
    rank = wid_at * hgt_size + hgt_at
    text_rows = lax.dynamic_slice_in_dim(results[4], rank * owned % grain, owned, 1)
    text_outs = [
        text_rows[0].astype(BF16),
        (text_rows[1] * SCALE).astype(BF16),
        (text_rows[2] * SCALE).astype(BF16),
        text_rows[3].astype(BF16),
    ]
    return tuple(latent + text_outs)


def solution(mesh):
    tiles = P("grp", "hgt", "wid", None)
    rows = P(("grp", "wid", "hgt"), None)
    return jax.shard_map(
        per_device,
        mesh=mesh,
        in_specs=(tiles,) * 4 + (P("grp", None),) * 4 + (P("grp"), P()),
        out_specs=(tiles,) * 4 + (rows,) * 4,
        check_vma=False,
    )
```

```python
import functools

import jax
import jax.numpy as jnp
from jax import lax
from jax.experimental import pallas as pl
from jax.experimental.pallas import tpu as pltpu
from jax.sharding import PartitionSpec as P

D = 128
SCALE = D ** (-0.5)
NEG = -1e30
F32 = jnp.float32
BF16 = jnp.bfloat16
def dot_nt(a, b):
    return lax.dot_general(a, b, (((1,), (1,)), ((), ())), preferred_element_type=F32)


def dot_nn(a, b):
    return lax.dot_general(a, b, (((1,), (0,)), ((), ())), preferred_element_type=F32)


def dot_tn(a, b):
    return lax.dot_general(a, b, (((0,), (0,)), ((), ())), preferred_element_type=F32)


def round_bf16(x):
    return x.astype(BF16).astype(F32)


def when(conds, run):
    conds = [c for c in conds if c is not None]
    if not conds:
        run()
        return
    total = conds[0]
    for c in conds[1:]:
        total = jnp.logical_and(total, c)
    pl.when(total)(run)


def neither(conds, run):
    conds = [c for c in conds if c is not None]
    if conds:
        total = conds[0]
        for c in conds[1:]:
            total = jnp.logical_and(total, c)
        pl.when(jnp.logical_not(total))(run)


def whole_kernel(
    wid_size,
    hgt_size,
    windows,
    latent_key,
    latent_value,
    latent_query,
    latent_grad,
    text_query_all,
    text_key_all,
    text_value_all,
    text_grad_all,
    text_bias,
    out0,
    out1,
    out2,
    out3,
    text_out,
    tiles,
    text_own,
    score,
    stats,
    text_stats,
    near_keys,
    self_keys,
    text_parts,
    text_landed,
    back,
    landed,
    load_sem,
    text_load_sem,
    half_send,
    half_recv,
    tile_send,
    tile_recv,
    stat_send,
    stat_recv,
    text_send,
    text_recv,
    part_send,
    part_recv,
    back_send,
    back_recv,
):
    outs = (out0, out1, out2, out3)
    count = tiles.shape[1]
    size, width = tiles.shape[2], tiles.shape[3]
    half = size // 2
    heads = width // D
    text = text_bias.shape[0]
    devices = wid_size * hgt_size
    tile_rows = hgt_size // 2
    tile_count = devices // 2
    grain = text_parts.shape[2]
    owned = text // devices

    wid, hgt = lax.axis_index("wid"), lax.axis_index("hgt")
    par = lax.rem(hgt, 2)
    row = hgt // 2
    rank = wid * hgt_size + hgt
    mine = pl.multiple_of(par * width, D)
    other = pl.multiple_of((1 - par) * width, D)
    tile_at = row * wid_size + wid
    mate = {"wid": wid, "hgt": hgt + 1 - 2 * par}

    def rank_peer(step):
        peer = lax.rem(rank + step, devices)
        return peer, {"wid": peer // hgt_size, "hgt": lax.rem(peer, hgt_size)}

    def tile_peer(step):
        peer = lax.rem(tile_at + step, tile_count)
        return {"wid": lax.rem(peer, wid_size), "hgt": 2 * (peer // wid_size) + par}

    def copy(src, dst, send, recv, device):
        return pltpu.make_async_remote_copy(
            src_ref=src,
            dst_ref=dst,
            send_sem=send,
            recv_sem=recv,
            device_id=device,
            device_id_type=pl.DeviceIdType.MESH,
        )

    has_left, has_right = wid > 0, wid < wid_size - 1
    left = {"wid": jnp.maximum(wid - 1, 0), "hgt": hgt}
    right = {"wid": jnp.minimum(wid + 1, wid_size - 1), "hgt": hgt}
    sides = [(1, right, has_right, has_left), (2, left, has_left, has_right)]
    if hgt_size == 4:
        uprights = [(1, {"wid": wid, "hgt": lax.rem(hgt + 2, 4)}, None, None)]
    else:
        has_up, has_down = row > 0, row < tile_rows - 1
        down = {"wid": wid, "hgt": jnp.minimum(hgt + 2, hgt_size - 2 + par)}
        up = {"wid": wid, "hgt": jnp.maximum(hgt - 2, par)}
        uprights = [(1, down, has_down, has_up), (2, up, has_up, has_down)]

    barrier = pltpu.get_barrier_semaphore()

    @pl.loop(1, devices)
    def _(step):
        _, device = rank_peer(step)
        pl.semaphore_signal(barrier, inc=1, device_id=device, device_id_type=pl.DeviceIdType.MESH)

    arrays = (latent_key, latent_value, latent_query, latent_grad)
    loads = [
        pltpu.make_async_copy(
            arrays[a].at[:, pl.ds(mine, width)], tiles.at[a, 0, pl.ds(0, half)], load_sem.at[a]
        )
        for a in range(4)
    ]
    for load in loads:
        load.start()
    text_loads = [
        pltpu.make_async_copy(
            array.at[:, pl.ds(mine, width)], text_own.at[a], text_load_sem.at[a]
        )
        for a, array in enumerate((text_query_all, text_key_all, text_value_all, text_grad_all))
    ]
    for load in text_loads:
        load.start()
    text_query, text_key, text_value, text_grad = (text_own.at[a] for a in range(4))

    self_gate = jnp.where(tile_at == 0, 0.0, NEG).astype(F32)
    gate_query, gate_key = [], []
    for dr in [0, 1 - 2 * row] if hgt_size == 4 else [0, -1, 1]:
        for dc in (0, -1, 1):
            near_row, near_col = row + dr, wid + dc
            inside = (near_row >= 0) & (near_row < tile_rows)
            inside = inside & (near_col >= 0) & (near_col < wid_size)
            near_row = jnp.clip(near_row, 0, tile_rows - 1)
            near_tile = near_row * wid_size + jnp.clip(near_col, 0, wid_size - 1)
            slot = (dr + 1) * 3 + dc + 1
            for gates, entry in (
                (gate_query, windows[tile_at, slot]),
                (gate_key, windows[near_tile, 8 - slot]),
            ):
                gates.append(jnp.where(inside & (entry >= 0), 0.0, NEG).astype(F32))
    pl.semaphore_wait(barrier, devices - 1)
    halves = [
        copy(
            arrays[a].at[:, pl.ds(other, width)],
            tiles.at[a, 0, pl.ds(half, half)],
            half_send.at[a],
            half_recv.at[a],
            mate,
        )
        for a in range(4)
    ]
    for move in halves:
        move.start()

    def hop(a, source, target, device):
        return copy(
            tiles.at[a, source],
            tiles.at[a, target],
            tile_send.at[a, target],
            tile_recv.at[a, target],
            device,
        )

    def stat_hop(source, target, device):
        return copy(
            stats.at[source],
            stats.at[target],
            stat_send.at[target],
            stat_recv.at[target],
            device,
        )

    sent = []

    def launch(make, conds):
        when(conds, lambda: make().start())
        sent.append((make, conds))

    def arrive(make, conds):
        when(conds, lambda: make().wait_recv())

    def upright_hops(a):
        for r, device, go, _ in uprights:
            launch(functools.partial(hop, a, 0, 3 * r, device), [go])

    def side_hops(a):
        for c, device, go, _ in sides:
            launch(functools.partial(hop, a, 0, c, device), [go])

    def second_hops(a):
        if a != 2:
            for r, device, _, come in uprights:
                arrive(lambda: hop(a, 0, 3 * r, device), [come])
            for r, _, _, come in uprights:
                for c, device, go, _ in sides:
                    launch(functools.partial(hop, a, 3 * r, 3 * r + c, device), [go, come])
        else:
            for c, device, _, come in sides:
                arrive(lambda: hop(a, 0, c, device), [come])
            for r, device, go, _ in uprights:
                for c, _, _, come in sides:
                    launch(functools.partial(hop, a, c, 3 * r + c, device), [go, come])

    def direct_arrived(a):
        if a != 2:
            for c, device, _, come in sides:
                arrive(lambda: hop(a, 0, c, device), [come])
        else:
            for r, device, _, come in uprights:
                arrive(lambda: hop(a, 0, 3 * r, device), [come])

    def corners_arrived(a):
        for r, _, _, come_row in uprights:
            for c, device, _, come in sides:
                arrive(lambda: hop(a, 0, 3 * r + c, device), [come, come_row])

    def clear(slot, conds):
        def run():
            for a in range(4):
                tiles[a, slot] = jnp.zeros((size, width), BF16)
            stats[slot] = jnp.zeros(stats.shape[1:], F32)

        neither(conds, run)

    for a in range(4):
        loads[a].wait()
        halves[a].wait_recv()
        if a < 2:
            upright_hops(a)
            side_hops(a)
    for c, _, _, come in sides:
        clear(c, [come])
    for r, _, _, come_row in uprights:
        clear(3 * r, [come_row])
        for c, _, _, come in sides:
            clear(3 * r + c, [come, come_row])

    def lanes(h):
        return pl.ds(pl.multiple_of(h * D, D), D)

    for load in text_loads:
        load.wait()

    def out_lanes(h):
        return pl.ds(pl.multiple_of(mine + h * D, D), D)

    def text_scores(h):
        query, grad = text_query[:, lanes(h)], text_grad[:, lanes(h)]
        near = dot_nt(tiles[0, 0, :, lanes(h)], query) * SCALE
        own = dot_nt(text_key[:, lanes(h)], query) * SCALE + (text_bias[...] + self_gate)
        dp_near = dot_nt(tiles[1, 0, :, lanes(h)], grad)
        dp_own = dot_nt(text_value[:, lanes(h)], grad)
        return query, grad, near, own, dp_near, dp_own

    @pl.loop(0, heads)
    def _(h):
        _, _, near, own, dp_near, dp_own = text_scores(h)
        top = jnp.maximum(
            jnp.max(near, axis=0, keepdims=True), jnp.max(own, axis=0, keepdims=True)
        )
        e_near = jnp.exp(near - top)
        e_own = jnp.exp(own - top)
        total = jnp.sum(e_near, axis=0, keepdims=True) + jnp.sum(e_own, axis=0, keepdims=True)
        mix = jnp.sum(e_near * dp_near, axis=0, keepdims=True) + jnp.sum(
            e_own * dp_own, axis=0, keepdims=True
        )
        text_stats[0, h] = jnp.concatenate(
            [top, total, mix, jnp.zeros((5, top.shape[1]), F32)], axis=0
        )

    def text_copy(step):
        return copy(
            text_stats.at[0],
            text_stats.at[step],
            text_send.at[step],
            text_recv.at[step],
            tile_peer(step),
        )

    @pl.loop(1, tile_count)
    def _(step):
        text_copy(step).start()

    second_hops(0)
    second_hops(1)
    upright_hops(2)
    upright_hops(3)

    @pl.loop(1, tile_count)
    def _(step):
        text_copy(step).wait_recv()

    def spread(at, h, value):
        text_parts[:, at, :, lanes(h)] = value.reshape(text // grain, grain, D).astype(BF16)

    @pl.loop(0, heads)
    def _(h):
        query, grad, near, own, dp_near, dp_own = text_scores(h)
        parts = text_stats[:, h]
        tops = parts[:, 0, :]
        top = jnp.max(tops, axis=0, keepdims=True)
        factor = jnp.exp(tops - top)
        total = jnp.sum(parts[:, 1, :] * factor, axis=0, keepdims=True)
        delta = jnp.sum(parts[:, 2, :] * factor, axis=0, keepdims=True) / total
        lse = top + jnp.log(total)
        p_near = jnp.exp(near - lse)
        p_own = jnp.exp(own - lse)
        low_near = p_near.astype(BF16)
        low_own = p_own.astype(BF16)
        ds_near = (p_near * (dp_near - delta)).astype(BF16)
        ds_own = (p_own * (dp_own - delta)).astype(BF16)
        spread(
            0,
            h,
            dot_tn(low_near, tiles[1, 0, :, lanes(h)])
            + dot_tn(low_own, text_value[:, lanes(h)]),
        )
        spread(
            1,
            h,
            dot_tn(ds_near, tiles[0, 0, :, lanes(h)]) + dot_tn(ds_own, text_key[:, lanes(h)]),
        )
        self_keys[0, :, lanes(h)] = dot_nn(ds_own, query)
        self_keys[1, :, lanes(h)] = dot_nn(low_own, grad)
        near_keys[0, :, lanes(h)] = dot_nn(ds_near, query)
        near_keys[1, :, lanes(h)] = dot_nn(low_near, grad)

    for a in range(2):
        direct_arrived(a)
    for a in range(2):
        corners_arrived(a)
    side_hops(2)
    side_hops(3)
    second_hops(3)

    spans = [(at * size, size) for at in range(count)] + [(count * size, text)]

    @pl.loop(0, heads)
    def _(h):
        @pl.when(h == heads // 2)
        def _():
            second_hops(2)

        query, grad = tiles[2, 0, :, lanes(h)], tiles[3, 0, :, lanes(h)]

        def key_of(at):
            return tiles[0, at, :, lanes(h)] if at < count else text_key[:, lanes(h)]

        def value_of(at):
            return tiles[1, at, :, lanes(h)] if at < count else text_value[:, lanes(h)]

        top = None
        for at, (first, length) in enumerate(spans):
            part = dot_nt(key_of(at), query) * SCALE
            part = part + (gate_query[at] if at < count else text_bias[...][:, :1])
            score[first : first + length] = part
            peak = jnp.max(part, axis=0, keepdims=True)
            top = peak if top is None else jnp.maximum(top, peak)
        shift = round_bf16(top)
        total = jnp.zeros_like(shift)
        for first, length in spans:
            weight = jnp.exp(score[first : first + length] - shift)
            score[first : first + length] = weight
            total = total + jnp.sum(weight, axis=0, keepdims=True)
        inverse = round_bf16(1.0 / total)
        out = jnp.zeros((D, size), F32)
        for at, (first, length) in enumerate(spans):
            low = (score[first : first + length] * inverse).astype(BF16)
            out = out + dot_tn(value_of(at), low)
            if at == count:
                spread(3, h, self_keys[1, :, lanes(h)] + dot_nn(low, grad))
        out = round_bf16(out)
        delta = round_bf16(jnp.sum(grad.astype(F32).T * out, axis=0, keepdims=True))
        query_grad = jnp.zeros((D, size), F32)
        for at, (first, length) in enumerate(spans):
            dp = dot_nt(value_of(at), grad)
            ds = (score[first : first + length] * inverse * (dp - delta)).astype(BF16)
            query_grad = query_grad + dot_tn(key_of(at), ds)
            if at == count:
                spread(2, h, self_keys[0, :, lanes(h)] + dot_nn(ds, query))
        for at, value in enumerate((out.T, (query_grad * SCALE).T)):
            value = value.astype(BF16)
            outs[at][:, out_lanes(h)] = value[:half]
            back[at, :, lanes(h)] = value[half:]
        stats[0, h] = jnp.concatenate([shift, inverse, delta, jnp.zeros((5, size), F32)], axis=0)

    for r, device, go, _ in uprights:
        launch(functools.partial(stat_hop, 0, 3 * r, device), [go])
    for c, device, go, _ in sides:
        launch(functools.partial(stat_hop, 0, c, device), [go])

    def part_copy(step):
        peer, device = rank_peer(step)
        return copy(
            text_parts.at[peer * owned // grain],
            text_landed.at[step],
            part_send.at[step],
            part_recv.at[step],
            device,
        )

    @pl.loop(1, devices)
    def _(step):
        part_copy(step).start()

    def back_copy(at):
        return copy(back.at[at], landed.at[at], back_send.at[at], back_recv.at[at], mate)

    for at in range(2):
        back_copy(at).start()

    for r, device, _, come in uprights:
        arrive(lambda: stat_hop(0, 3 * r, device), [come])
    for r, _, _, come in uprights:
        for c, device, go, _ in sides:
            launch(functools.partial(stat_hop, 3 * r, 3 * r + c, device), [go, come])
    for c, device, _, come in sides:
        arrive(lambda: stat_hop(0, c, device), [come])
    direct_arrived(2)
    direct_arrived(3)

    def key_part(h, slots):
        key, value = tiles[0, 0, :, lanes(h)], tiles[1, 0, :, lanes(h)]
        key_grad = near_keys[0, :, lanes(h)]
        value_grad = near_keys[1, :, lanes(h)]
        for at in slots:
            query, grad = tiles[2, at, :, lanes(h)], tiles[3, at, :, lanes(h)]
            rows = stats[at, h]
            shift, inverse, delta = rows[0:1], rows[1:2], rows[2:3]
            prob = jnp.exp(dot_nt(key, query) * SCALE + (gate_key[at] - shift)) * inverse
            ds = (prob * (dot_nt(value, grad) - delta)).astype(BF16)
            value_grad = value_grad + dot_nn(prob.astype(BF16), grad)
            key_grad = key_grad + dot_nn(ds, query)
        return key_grad, value_grad

    corners = [3 * r + c for r, _, _, _ in uprights for c in (1, 2)]

    @pl.loop(0, heads)
    def _(h):
        key_grad, value_grad = key_part(h, [at for at in range(count) if at not in corners])
        near_keys[0, :, lanes(h)] = key_grad
        near_keys[1, :, lanes(h)] = value_grad

    for r, _, _, come_row in uprights:
        for c, device, _, come in sides:
            arrive(lambda: stat_hop(0, 3 * r + c, device), [come, come_row])
    corners_arrived(2)
    corners_arrived(3)

    @pl.loop(0, heads)
    def _(h):
        key_grad, value_grad = key_part(h, corners)
        for at, grads in ((2, key_grad * SCALE), (3, value_grad)):
            grads = grads.astype(BF16)
            outs[at][:, out_lanes(h)] = grads[:half]
            back[at, :, lanes(h)] = grads[half:]

    for at in range(2, 4):
        back_copy(at).start()

    @pl.loop(1, devices)
    def _(step):
        part_copy(step).wait_recv()

    own_part = text_parts[rank * owned // grain].astype(F32)

    def add_pair(step, sums):
        same = sums[0] + text_landed[2 * step].astype(F32)
        return same, sums[1] + text_landed[2 * step + 1].astype(F32)

    same, cross = lax.fori_loop(
        1, devices // 2, add_pair, (own_part, text_landed[1].astype(F32))
    )
    text_out[:, :, pl.ds(mine, width)] = same
    text_out[:, :, pl.ds(other, width)] = cross

    for at in range(4):
        back_copy(at).wait_recv()
        outs[at][:, pl.ds(other, width)] = landed[at]

    for move in halves:
        move.wait_send()
    for make, conds in sent:
        when(conds, lambda: make().wait_send())

    @pl.loop(1, tile_count)
    def _(step):
        text_copy(step).wait_send()

    @pl.loop(1, devices)
    def _(step):
        part_copy(step).wait_send()

    for at in range(4):
        back_copy(at).wait_send()


def finish_kernel(owned, grain, hgt_size, *refs):
    ins, text_sums = refs[:4], refs[4]
    outs, text_outs, sems = refs[5:9], refs[9:13], refs[13]
    moves = [pltpu.make_async_copy(ins[a], outs[a], sems.at[a]) for a in range(4)]
    for move in moves:
        move.start()
    rank = lax.axis_index("wid") * hgt_size + lax.axis_index("hgt")
    first = 0 if owned == grain else lax.rem(rank * owned, grain)
    for a in range(4):
        sums = text_sums[a, pl.ds(first, owned), :]
        text_outs[a][...] = (sums * SCALE if a in (1, 2) else sums).astype(BF16)
    for move in moves:
        move.wait()


def per_device(
    latent_query,
    latent_key,
    latent_value,
    latent_grad,
    text_query,
    text_key,
    text_value,
    text_grad,
    text_valid,
    windows,
):
    block = latent_query.shape
    channels = block[3]
    rows = block[0] * block[1] * block[2]
    size = 2 * rows
    width = channels // 2
    heads = width // D
    text = text_query.shape[0]
    wid_size, hgt_size = lax.axis_size("wid"), lax.axis_size("hgt")
    devices = wid_size * hgt_size
    count = 6 if hgt_size == 4 else 9
    text_bias = jnp.broadcast_to(
        jnp.where(text_valid == 1, 0.0, NEG).astype(F32)[:, None], (text, text)
    )
    owned = text // devices
    grain = max(owned, 8)
    flat = [a.reshape(rows, channels) for a in (latent_key, latent_value, latent_query, latent_grad)]
    smem = pl.BlockSpec(memory_space=pltpu.SMEM)
    hbm = pl.BlockSpec(memory_space=pl.ANY)
    vmem = pl.BlockSpec(memory_space=pltpu.VMEM)
    dma = pltpu.SemaphoreType.DMA
    whole = jax.ShapeDtypeStruct((rows, channels), BF16)
    results = pl.pallas_call(
        functools.partial(whole_kernel, wid_size, hgt_size),
        in_specs=[smem] + [hbm] * 8 + [vmem],
        out_specs=[vmem] * 5,
        out_shape=[whole] * 4 + [jax.ShapeDtypeStruct((4, grain, channels), F32)],
        scratch_shapes=[
            pltpu.VMEM((4, count, size, width), BF16),
            pltpu.VMEM((4, text, width), BF16),
            pltpu.VMEM((count * size + text, size), F32),
            pltpu.VMEM((count, heads, 8, size), F32),
            pltpu.VMEM((devices // 2, heads, 8, text), F32),
            pltpu.VMEM((2, size, width), F32),
            pltpu.VMEM((2, text, width), F32),
            pltpu.VMEM((text // grain, 4, grain, width), BF16),
            pltpu.VMEM((devices, 4, grain, width), BF16),
            pltpu.VMEM((4, rows, width), BF16),
            pltpu.VMEM((4, rows, width), BF16),
            dma((4,)),
            dma((4,)),
            dma((4,)),
            dma((4,)),
            dma((4, count)),
            dma((4, count)),
            dma((count,)),
            dma((count,)),
            dma((devices // 2,)),
            dma((devices // 2,)),
            dma((devices,)),
            dma((devices,)),
            dma((4,)),
            dma((4,)),
        ],
        compiler_params=pltpu.CompilerParams(
            collective_id=0, has_side_effects=True, vmem_limit_bytes=56 * 1024 * 1024
        ),
        name="joint_attention",
    )(windows, *flat, text_query, text_key, text_value, text_grad, text_bias)
    finished = pl.pallas_call(
        functools.partial(finish_kernel, owned, grain, hgt_size),
        in_specs=[hbm] * 4 + [vmem],
        out_specs=[hbm] * 4 + [vmem] * 4,
        out_shape=[whole] * 4 + [jax.ShapeDtypeStruct((owned, channels), BF16)] * 4,
        scratch_shapes=[dma((4,))],
        name="finish",
    )(*results)
    return tuple([a.reshape(block) for a in finished[:4]] + list(finished[4:]))


def solution(mesh):
    tiles = P("grp", "hgt", "wid", None)
    rows = P(("grp", "wid", "hgt"), None)
    return jax.shard_map(
        per_device,
        mesh=mesh,
        in_specs=(tiles,) * 4 + (P("grp", None),) * 4 + (P("grp"), P()),
        out_specs=(tiles,) * 4 + (rows,) * 4,
        check_vma=False,
    )
```

```python
import functools

import jax
import jax.numpy as jnp
from jax import lax
from jax.experimental import pallas as pl
from jax.experimental.pallas import tpu as pltpu
from jax.sharding import PartitionSpec as P

D = 128
SCALE = D ** (-0.5)
NEG = -1e30
F32 = jnp.float32
BF16 = jnp.bfloat16
def dot_nt(a, b):
    return lax.dot_general(a, b, (((1,), (1,)), ((), ())), preferred_element_type=F32)


def dot_nn(a, b):
    return lax.dot_general(a, b, (((1,), (0,)), ((), ())), preferred_element_type=F32)


def dot_tn(a, b):
    return lax.dot_general(a, b, (((0,), (0,)), ((), ())), preferred_element_type=F32)


def round_bf16(x):
    return x.astype(BF16).astype(F32)


def when(conds, run):
    conds = [c for c in conds if c is not None]
    if not conds:
        run()
        return
    total = conds[0]
    for c in conds[1:]:
        total = jnp.logical_and(total, c)
    pl.when(total)(run)


def neither(conds, run):
    conds = [c for c in conds if c is not None]
    if conds:
        total = conds[0]
        for c in conds[1:]:
            total = jnp.logical_and(total, c)
        pl.when(jnp.logical_not(total))(run)


def whole_kernel(
    wid_size,
    hgt_size,
    windows,
    latent_key,
    latent_value,
    latent_query,
    latent_grad,
    text_query_all,
    text_key_all,
    text_value_all,
    text_grad_all,
    text_bias,
    out0,
    out1,
    out2,
    out3,
    text_out,
    tiles,
    text_own,
    score,
    stats,
    text_stats,
    near_keys,
    self_keys,
    text_parts,
    text_landed,
    back,
    landed,
    load_sem,
    text_load_sem,
    half_send,
    half_recv,
    tile_send,
    tile_recv,
    stat_send,
    stat_recv,
    text_send,
    text_recv,
    part_send,
    part_recv,
    back_send,
    back_recv,
):
    outs = (out0, out1, out2, out3)
    count = tiles.shape[1]
    size, width = tiles.shape[2], tiles.shape[3]
    half = size // 2
    heads = width // D
    text = text_bias.shape[0]
    devices = wid_size * hgt_size
    tile_rows = hgt_size // 2
    tile_count = devices // 2
    grain = text_parts.shape[2]
    owned = text // devices

    wid, hgt = lax.axis_index("wid"), lax.axis_index("hgt")
    par = lax.rem(hgt, 2)
    row = hgt // 2
    rank = wid * hgt_size + hgt
    mine = pl.multiple_of(par * width, D)
    other = pl.multiple_of((1 - par) * width, D)
    tile_at = row * wid_size + wid
    mate = {"wid": wid, "hgt": hgt + 1 - 2 * par}

    def rank_peer(step):
        peer = lax.rem(rank + step, devices)
        return peer, {"wid": peer // hgt_size, "hgt": lax.rem(peer, hgt_size)}

    def tile_peer(step):
        peer = lax.rem(tile_at + step, tile_count)
        return {"wid": lax.rem(peer, wid_size), "hgt": 2 * (peer // wid_size) + par}

    def copy(src, dst, send, recv, device):
        return pltpu.make_async_remote_copy(
            src_ref=src,
            dst_ref=dst,
            send_sem=send,
            recv_sem=recv,
            device_id=device,
            device_id_type=pl.DeviceIdType.MESH,
        )

    has_left, has_right = wid > 0, wid < wid_size - 1
    left = {"wid": jnp.maximum(wid - 1, 0), "hgt": hgt}
    right = {"wid": jnp.minimum(wid + 1, wid_size - 1), "hgt": hgt}
    sides = [(1, right, has_right, has_left), (2, left, has_left, has_right)]
    if hgt_size == 4:
        uprights = [(1, {"wid": wid, "hgt": lax.rem(hgt + 2, 4)}, None, None)]
    else:
        has_up, has_down = row > 0, row < tile_rows - 1
        down = {"wid": wid, "hgt": jnp.minimum(hgt + 2, hgt_size - 2 + par)}
        up = {"wid": wid, "hgt": jnp.maximum(hgt - 2, par)}
        uprights = [(1, down, has_down, has_up), (2, up, has_up, has_down)]

    barrier = pltpu.get_barrier_semaphore()

    @pl.loop(1, devices)
    def _(step):
        _, device = rank_peer(step)
        pl.semaphore_signal(barrier, inc=1, device_id=device, device_id_type=pl.DeviceIdType.MESH)

    arrays = (latent_key, latent_value, latent_query, latent_grad)
    loads = [
        pltpu.make_async_copy(
            arrays[a].at[:, pl.ds(mine, width)], tiles.at[a, 0, pl.ds(0, half)], load_sem.at[a]
        )
        for a in range(4)
    ]
    for load in loads:
        load.start()
    text_loads = [
        pltpu.make_async_copy(
            array.at[:, pl.ds(mine, width)], text_own.at[a], text_load_sem.at[a]
        )
        for a, array in enumerate((text_query_all, text_key_all, text_value_all, text_grad_all))
    ]
    for load in text_loads:
        load.start()
    text_query, text_key, text_value, text_grad = (text_own.at[a] for a in range(4))

    self_gate = jnp.where(tile_at == 0, 0.0, NEG).astype(F32)
    gate_query, gate_key = [], []
    for dr in [0, 1 - 2 * row] if hgt_size == 4 else [0, -1, 1]:
        for dc in (0, -1, 1):
            near_row, near_col = row + dr, wid + dc
            inside = (near_row >= 0) & (near_row < tile_rows)
            inside = inside & (near_col >= 0) & (near_col < wid_size)
            near_row = jnp.clip(near_row, 0, tile_rows - 1)
            near_tile = near_row * wid_size + jnp.clip(near_col, 0, wid_size - 1)
            slot = (dr + 1) * 3 + dc + 1
            for gates, entry in (
                (gate_query, windows[tile_at, slot]),
                (gate_key, windows[near_tile, 8 - slot]),
            ):
                gates.append(jnp.where(inside & (entry >= 0), 0.0, NEG).astype(F32))
    pl.semaphore_wait(barrier, devices - 1)
    halves = [
        copy(
            arrays[a].at[:, pl.ds(other, width)],
            tiles.at[a, 0, pl.ds(half, half)],
            half_send.at[a],
            half_recv.at[a],
            mate,
        )
        for a in range(4)
    ]
    for move in halves:
        move.start()

    def hop(a, source, target, device):
        return copy(
            tiles.at[a, source],
            tiles.at[a, target],
            tile_send.at[a, target],
            tile_recv.at[a, target],
            device,
        )

    def stat_hop(source, target, device):
        return copy(
            stats.at[source],
            stats.at[target],
            stat_send.at[target],
            stat_recv.at[target],
            device,
        )

    sent = []

    def launch(make, conds):
        when(conds, lambda: make().start())
        sent.append((make, conds))

    def arrive(make, conds):
        when(conds, lambda: make().wait_recv())

    def upright_hops(a):
        for r, device, go, _ in uprights:
            launch(functools.partial(hop, a, 0, 3 * r, device), [go])

    def side_hops(a):
        for c, device, go, _ in sides:
            launch(functools.partial(hop, a, 0, c, device), [go])

    def routes(a):
        if a == 1:
            return [(True, par == 0), (False, par == 1)]
        return [(a == 2, None)]

    def second_hops(a):
        for by_side_first, use in routes(a):
            if by_side_first:
                for c, device, _, come in sides:
                    arrive(functools.partial(hop, a, 0, c, device), [come, use])
                for r, device, go, _ in uprights:
                    for c, _, _, come in sides:
                        launch(functools.partial(hop, a, c, 3 * r + c, device), [go, come, use])
            else:
                for r, device, _, come in uprights:
                    arrive(functools.partial(hop, a, 0, 3 * r, device), [come, use])
                for r, _, _, come in uprights:
                    for c, device, go, _ in sides:
                        launch(
                            functools.partial(hop, a, 3 * r, 3 * r + c, device), [go, come, use]
                        )

    def direct_arrived(a):
        for by_side_first, use in routes(a):
            if by_side_first:
                for r, device, _, come in uprights:
                    arrive(functools.partial(hop, a, 0, 3 * r, device), [come, use])
            else:
                for c, device, _, come in sides:
                    arrive(functools.partial(hop, a, 0, c, device), [come, use])

    def corners_arrived(a):
        for r, _, _, come_row in uprights:
            for c, device, _, come in sides:
                arrive(lambda: hop(a, 0, 3 * r + c, device), [come, come_row])

    def clear(slot, conds):
        def run():
            for a in range(4):
                tiles[a, slot] = jnp.zeros((size, width), BF16)
            stats[slot] = jnp.zeros(stats.shape[1:], F32)

        neither(conds, run)

    for a in range(4):
        loads[a].wait()
        halves[a].wait_recv()
        if a < 2:
            upright_hops(a)
            side_hops(a)
    for c, _, _, come in sides:
        clear(c, [come])
    for r, _, _, come_row in uprights:
        clear(3 * r, [come_row])
        for c, _, _, come in sides:
            clear(3 * r + c, [come, come_row])

    def lanes(h):
        return pl.ds(pl.multiple_of(h * D, D), D)

    for load in text_loads:
        load.wait()

    def out_lanes(h):
        return pl.ds(pl.multiple_of(mine + h * D, D), D)

    def text_scores(h):
        query, grad = text_query[:, lanes(h)], text_grad[:, lanes(h)]
        near = dot_nt(tiles[0, 0, :, lanes(h)], query) * SCALE
        own = dot_nt(text_key[:, lanes(h)], query) * SCALE + (text_bias[...] + self_gate)
        dp_near = dot_nt(tiles[1, 0, :, lanes(h)], grad)
        dp_own = dot_nt(text_value[:, lanes(h)], grad)
        return query, grad, near, own, dp_near, dp_own

    @pl.loop(0, heads)
    def _(h):
        _, _, near, own, dp_near, dp_own = text_scores(h)
        top = jnp.maximum(
            jnp.max(near, axis=0, keepdims=True), jnp.max(own, axis=0, keepdims=True)
        )
        e_near = jnp.exp(near - top)
        e_own = jnp.exp(own - top)
        total = jnp.sum(e_near, axis=0, keepdims=True) + jnp.sum(e_own, axis=0, keepdims=True)
        mix = jnp.sum(e_near * dp_near, axis=0, keepdims=True) + jnp.sum(
            e_own * dp_own, axis=0, keepdims=True
        )
        text_stats[0, h] = jnp.concatenate(
            [top, total, mix, jnp.zeros((5, top.shape[1]), F32)], axis=0
        )

    def text_copy(step):
        return copy(
            text_stats.at[0],
            text_stats.at[step],
            text_send.at[step],
            text_recv.at[step],
            tile_peer(step),
        )

    @pl.loop(1, tile_count)
    def _(step):
        text_copy(step).start()

    second_hops(0)
    second_hops(1)
    upright_hops(2)
    upright_hops(3)

    @pl.loop(1, tile_count)
    def _(step):
        text_copy(step).wait_recv()

    def spread(at, h, value):
        text_parts[:, at, :, lanes(h)] = value.reshape(text // grain, grain, D).astype(BF16)

    @pl.loop(0, heads)
    def _(h):
        query, grad, near, own, dp_near, dp_own = text_scores(h)
        parts = text_stats[:, h]
        tops = parts[:, 0, :]
        top = jnp.max(tops, axis=0, keepdims=True)
        factor = jnp.exp(tops - top)
        total = jnp.sum(parts[:, 1, :] * factor, axis=0, keepdims=True)
        delta = jnp.sum(parts[:, 2, :] * factor, axis=0, keepdims=True) / total
        lse = top + jnp.log(total)
        p_near = jnp.exp(near - lse)
        p_own = jnp.exp(own - lse)
        low_near = p_near.astype(BF16)
        low_own = p_own.astype(BF16)
        ds_near = (p_near * (dp_near - delta)).astype(BF16)
        ds_own = (p_own * (dp_own - delta)).astype(BF16)
        spread(
            0,
            h,
            dot_tn(low_near, tiles[1, 0, :, lanes(h)])
            + dot_tn(low_own, text_value[:, lanes(h)]),
        )
        spread(
            1,
            h,
            dot_tn(ds_near, tiles[0, 0, :, lanes(h)]) + dot_tn(ds_own, text_key[:, lanes(h)]),
        )
        self_keys[0, :, lanes(h)] = dot_nn(ds_own, query)
        self_keys[1, :, lanes(h)] = dot_nn(low_own, grad)
        near_keys[0, :, lanes(h)] = dot_nn(ds_near, query)
        near_keys[1, :, lanes(h)] = dot_nn(low_near, grad)

    for a in range(2):
        direct_arrived(a)
    for a in range(2):
        corners_arrived(a)
    side_hops(2)
    side_hops(3)
    second_hops(3)

    spans = [(at * size, size) for at in range(count)] + [(count * size, text)]

    @pl.loop(0, heads)
    def _(h):
        @pl.when(h == heads // 2)
        def _():
            second_hops(2)

        query, grad = tiles[2, 0, :, lanes(h)], tiles[3, 0, :, lanes(h)]

        def key_of(at):
            return tiles[0, at, :, lanes(h)] if at < count else text_key[:, lanes(h)]

        def value_of(at):
            return tiles[1, at, :, lanes(h)] if at < count else text_value[:, lanes(h)]

        top = None
        for at, (first, length) in enumerate(spans):
            part = dot_nt(key_of(at), query) * SCALE
            part = part + (gate_query[at] if at < count else text_bias[...][:, :1])
            score[first : first + length] = part
            peak = jnp.max(part, axis=0, keepdims=True)
            top = peak if top is None else jnp.maximum(top, peak)
        shift = round_bf16(top)
        total = jnp.zeros_like(shift)
        for first, length in spans:
            weight = jnp.exp(score[first : first + length] - shift)
            score[first : first + length] = weight
            total = total + jnp.sum(weight, axis=0, keepdims=True)
        inverse = round_bf16(1.0 / total)
        out = jnp.zeros((D, size), F32)
        for at, (first, length) in enumerate(spans):
            low = (score[first : first + length] * inverse).astype(BF16)
            out = out + dot_tn(value_of(at), low)
            if at == count:
                spread(3, h, self_keys[1, :, lanes(h)] + dot_nn(low, grad))
        out = round_bf16(out)
        delta = round_bf16(jnp.sum(grad.astype(F32).T * out, axis=0, keepdims=True))
        query_grad = jnp.zeros((D, size), F32)
        for at, (first, length) in enumerate(spans):
            dp = dot_nt(value_of(at), grad)
            ds = (score[first : first + length] * inverse * (dp - delta)).astype(BF16)
            query_grad = query_grad + dot_tn(key_of(at), ds)
            if at == count:
                spread(2, h, self_keys[0, :, lanes(h)] + dot_nn(ds, query))
        for at, value in enumerate((out.T, (query_grad * SCALE).T)):
            value = value.astype(BF16)
            outs[at][:, out_lanes(h)] = value[:half]
            back[at, :, lanes(h)] = value[half:]
        stats[0, h] = jnp.concatenate([shift, inverse, delta, jnp.zeros((5, size), F32)], axis=0)

    for r, device, go, _ in uprights:
        launch(functools.partial(stat_hop, 0, 3 * r, device), [go])
    for c, device, go, _ in sides:
        launch(functools.partial(stat_hop, 0, c, device), [go])

    def part_copy(step):
        peer, device = rank_peer(step)
        return copy(
            text_parts.at[peer * owned // grain],
            text_landed.at[step],
            part_send.at[step],
            part_recv.at[step],
            device,
        )

    @pl.loop(1, devices)
    def _(step):
        part_copy(step).start()

    def back_copy(at):
        return copy(back.at[at], landed.at[at], back_send.at[at], back_recv.at[at], mate)

    for at in range(2):
        back_copy(at).start()

    for r, device, _, come in uprights:
        arrive(lambda: stat_hop(0, 3 * r, device), [come])
    for r, _, _, come in uprights:
        for c, device, go, _ in sides:
            launch(functools.partial(stat_hop, 3 * r, 3 * r + c, device), [go, come])
    for c, device, _, come in sides:
        arrive(lambda: stat_hop(0, c, device), [come])
    direct_arrived(2)
    direct_arrived(3)

    def key_part(h, slots):
        key, value = tiles[0, 0, :, lanes(h)], tiles[1, 0, :, lanes(h)]
        key_grad = near_keys[0, :, lanes(h)]
        value_grad = near_keys[1, :, lanes(h)]
        for at in slots:
            query, grad = tiles[2, at, :, lanes(h)], tiles[3, at, :, lanes(h)]
            rows = stats[at, h]
            shift, inverse, delta = rows[0:1], rows[1:2], rows[2:3]
            prob = jnp.exp(dot_nt(key, query) * SCALE + (gate_key[at] - shift)) * inverse
            ds = (prob * (dot_nt(value, grad) - delta)).astype(BF16)
            value_grad = value_grad + dot_nn(prob.astype(BF16), grad)
            key_grad = key_grad + dot_nn(ds, query)
        return key_grad, value_grad

    corners = [3 * r + c for r, _, _, _ in uprights for c in (1, 2)]

    @pl.loop(0, heads)
    def _(h):
        key_grad, value_grad = key_part(h, [at for at in range(count) if at not in corners])
        near_keys[0, :, lanes(h)] = key_grad
        near_keys[1, :, lanes(h)] = value_grad

    for r, _, _, come_row in uprights:
        for c, device, _, come in sides:
            arrive(lambda: stat_hop(0, 3 * r + c, device), [come, come_row])
    corners_arrived(2)
    corners_arrived(3)

    @pl.loop(0, heads)
    def _(h):
        key_grad, value_grad = key_part(h, corners)
        for at, grads in ((2, key_grad * SCALE), (3, value_grad)):
            grads = grads.astype(BF16)
            outs[at][:, out_lanes(h)] = grads[:half]
            back[at, :, lanes(h)] = grads[half:]

    for at in range(2, 4):
        back_copy(at).start()

    @pl.loop(1, devices)
    def _(step):
        part_copy(step).wait_recv()

    own_part = text_parts[rank * owned // grain].astype(F32)

    def add_pair(step, sums):
        same = sums[0] + text_landed[2 * step].astype(F32)
        return same, sums[1] + text_landed[2 * step + 1].astype(F32)

    same, cross = lax.fori_loop(
        1, devices // 2, add_pair, (own_part, text_landed[1].astype(F32))
    )
    text_out[:, :, pl.ds(mine, width)] = same
    text_out[:, :, pl.ds(other, width)] = cross

    for at in range(4):
        back_copy(at).wait_recv()
        outs[at][:, pl.ds(other, width)] = landed[at]

    for move in halves:
        move.wait_send()
    for make, conds in sent:
        when(conds, lambda: make().wait_send())

    @pl.loop(1, tile_count)
    def _(step):
        text_copy(step).wait_send()

    @pl.loop(1, devices)
    def _(step):
        part_copy(step).wait_send()

    for at in range(4):
        back_copy(at).wait_send()


def finish_kernel(owned, grain, hgt_size, *refs):
    ins, text_sums = refs[:4], refs[4]
    outs, text_outs = refs[5:9], refs[9:13]
    for a in range(4):
        outs[a][...] = ins[a][...]
    rank = lax.axis_index("wid") * hgt_size + lax.axis_index("hgt")
    first = 0 if owned == grain else lax.rem(rank * owned, grain)
    for a in range(4):
        sums = text_sums[a, pl.ds(first, owned), :]
        text_outs[a][...] = (sums * SCALE if a in (1, 2) else sums).astype(BF16)


def per_device(
    latent_query,
    latent_key,
    latent_value,
    latent_grad,
    text_query,
    text_key,
    text_value,
    text_grad,
    text_valid,
    windows,
):
    block = latent_query.shape
    channels = block[3]
    rows = block[0] * block[1] * block[2]
    size = 2 * rows
    width = channels // 2
    heads = width // D
    text = text_query.shape[0]
    wid_size, hgt_size = lax.axis_size("wid"), lax.axis_size("hgt")
    devices = wid_size * hgt_size
    count = 6 if hgt_size == 4 else 9
    text_bias = jnp.broadcast_to(
        jnp.where(text_valid == 1, 0.0, NEG).astype(F32)[:, None], (text, text)
    )
    owned = text // devices
    grain = max(owned, 8)
    flat = [a.reshape(rows, channels) for a in (latent_key, latent_value, latent_query, latent_grad)]
    smem = pl.BlockSpec(memory_space=pltpu.SMEM)
    hbm = pl.BlockSpec(memory_space=pl.ANY)
    vmem = pl.BlockSpec(memory_space=pltpu.VMEM)
    dma = pltpu.SemaphoreType.DMA
    whole = jax.ShapeDtypeStruct((rows, channels), BF16)
    results = pl.pallas_call(
        functools.partial(whole_kernel, wid_size, hgt_size),
        in_specs=[smem] + [hbm] * 8 + [vmem],
        out_specs=[vmem] * 5,
        out_shape=[whole] * 4 + [jax.ShapeDtypeStruct((4, grain, channels), F32)],
        scratch_shapes=[
            pltpu.VMEM((4, count, size, width), BF16),
            pltpu.VMEM((4, text, width), BF16),
            pltpu.VMEM((count * size + text, size), F32),
            pltpu.VMEM((count, heads, 8, size), F32),
            pltpu.VMEM((devices // 2, heads, 8, text), F32),
            pltpu.VMEM((2, size, width), F32),
            pltpu.VMEM((2, text, width), F32),
            pltpu.VMEM((text // grain, 4, grain, width), BF16),
            pltpu.VMEM((devices, 4, grain, width), BF16),
            pltpu.VMEM((4, rows, width), BF16),
            pltpu.VMEM((4, rows, width), BF16),
            dma((4,)),
            dma((4,)),
            dma((4,)),
            dma((4,)),
            dma((4, count)),
            dma((4, count)),
            dma((count,)),
            dma((count,)),
            dma((devices // 2,)),
            dma((devices // 2,)),
            dma((devices,)),
            dma((devices,)),
            dma((4,)),
            dma((4,)),
        ],
        compiler_params=pltpu.CompilerParams(
            collective_id=0, has_side_effects=True, vmem_limit_bytes=56 * 1024 * 1024
        ),
        name="joint_attention",
    )(windows, *flat, text_query, text_key, text_value, text_grad, text_bias)
    finished = pl.pallas_call(
        functools.partial(finish_kernel, owned, grain, hgt_size),
        in_specs=[vmem] * 5,
        out_specs=[vmem] * 8,
        out_shape=[whole] * 4 + [jax.ShapeDtypeStruct((owned, channels), BF16)] * 4,
        name="finish",
    )(*results)
    return tuple([a.reshape(block) for a in finished[:4]] + list(finished[4:]))


def solution(mesh):
    tiles = P("grp", "hgt", "wid", None)
    rows = P(("grp", "wid", "hgt"), None)
    return jax.shard_map(
        per_device,
        mesh=mesh,
        in_specs=(tiles,) * 4 + (P("grp", None),) * 4 + (P("grp"), P()),
        out_specs=(tiles,) * 4 + (rows,) * 4,
        check_vma=False,
    )
```

```python
import functools

import jax
import jax.numpy as jnp
from jax import lax
from jax.experimental import pallas as pl
from jax.experimental.pallas import tpu as pltpu
from jax.sharding import PartitionSpec as P

D = 128
SCALE = D ** (-0.5)
NEG = -1e30
F32 = jnp.float32
BF16 = jnp.bfloat16
def dot_nt(a, b):
    return lax.dot_general(a, b, (((1,), (1,)), ((), ())), preferred_element_type=F32)


def dot_nn(a, b):
    return lax.dot_general(a, b, (((1,), (0,)), ((), ())), preferred_element_type=F32)


def dot_tn(a, b):
    return lax.dot_general(a, b, (((0,), (0,)), ((), ())), preferred_element_type=F32)


def round_bf16(x):
    return x.astype(BF16).astype(F32)


def when(conds, run):
    conds = [c for c in conds if c is not None]
    if not conds:
        run()
        return
    total = conds[0]
    for c in conds[1:]:
        total = jnp.logical_and(total, c)
    pl.when(total)(run)


def neither(conds, run):
    conds = [c for c in conds if c is not None]
    if conds:
        total = conds[0]
        for c in conds[1:]:
            total = jnp.logical_and(total, c)
        pl.when(jnp.logical_not(total))(run)


def whole_kernel(
    wid_size,
    hgt_size,
    windows,
    latent_key,
    latent_value,
    latent_query,
    latent_grad,
    text_query_all,
    text_key_all,
    text_value_all,
    text_grad_all,
    text_bias,
    out0,
    out1,
    out2,
    out3,
    text_out,
    tiles,
    text_own,
    score,
    stats,
    text_stats,
    near_keys,
    self_keys,
    text_parts,
    text_landed,
    back,
    landed,
    load_sem,
    text_load_sem,
    half_send,
    half_recv,
    tile_send,
    tile_recv,
    stat_send,
    stat_recv,
    text_send,
    text_recv,
    part_send,
    part_recv,
    back_send,
    back_recv,
):
    outs = (out0, out1, out2, out3)
    count = tiles.shape[1]
    size, width = tiles.shape[2], tiles.shape[3]
    half = size // 2
    heads = width // D
    text = text_bias.shape[0]
    devices = wid_size * hgt_size
    tile_rows = hgt_size // 2
    tile_count = devices // 2
    grain = text_parts.shape[2]
    owned = text // devices

    wid, hgt = lax.axis_index("wid"), lax.axis_index("hgt")
    par = lax.rem(hgt, 2)
    row = hgt // 2
    rank = wid * hgt_size + hgt
    mine = pl.multiple_of(par * width, D)
    other = pl.multiple_of((1 - par) * width, D)
    tile_at = row * wid_size + wid
    mate = {"wid": wid, "hgt": hgt + 1 - 2 * par}

    def rank_peer(step):
        peer = lax.rem(rank + step, devices)
        return peer, {"wid": peer // hgt_size, "hgt": lax.rem(peer, hgt_size)}

    def tile_peer(step):
        peer = lax.rem(tile_at + step, tile_count)
        return {"wid": lax.rem(peer, wid_size), "hgt": 2 * (peer // wid_size) + par}

    def copy(src, dst, send, recv, device):
        return pltpu.make_async_remote_copy(
            src_ref=src,
            dst_ref=dst,
            send_sem=send,
            recv_sem=recv,
            device_id=device,
            device_id_type=pl.DeviceIdType.MESH,
        )

    has_left, has_right = wid > 0, wid < wid_size - 1
    left = {"wid": jnp.maximum(wid - 1, 0), "hgt": hgt}
    right = {"wid": jnp.minimum(wid + 1, wid_size - 1), "hgt": hgt}
    sides = [(1, right, has_right, has_left), (2, left, has_left, has_right)]
    if hgt_size == 4:
        uprights = [(1, {"wid": wid, "hgt": lax.rem(hgt + 2, 4)}, None, None)]
    else:
        has_up, has_down = row > 0, row < tile_rows - 1
        down = {"wid": wid, "hgt": jnp.minimum(hgt + 2, hgt_size - 2 + par)}
        up = {"wid": wid, "hgt": jnp.maximum(hgt - 2, par)}
        uprights = [(1, down, has_down, has_up), (2, up, has_up, has_down)]

    barrier = pltpu.get_barrier_semaphore()

    @pl.loop(1, devices)
    def _(step):
        _, device = rank_peer(step)
        pl.semaphore_signal(barrier, inc=1, device_id=device, device_id_type=pl.DeviceIdType.MESH)

    arrays = (latent_key, latent_value, latent_query, latent_grad)
    loads = [
        pltpu.make_async_copy(
            arrays[a].at[:, pl.ds(mine, width)], tiles.at[a, 0, pl.ds(0, half)], load_sem.at[a]
        )
        for a in range(4)
    ]
    for load in loads:
        load.start()
    text_loads = [
        pltpu.make_async_copy(
            array.at[:, pl.ds(mine, width)], text_own.at[a], text_load_sem.at[a]
        )
        for a, array in enumerate((text_query_all, text_key_all, text_value_all, text_grad_all))
    ]
    for load in text_loads:
        load.start()
    text_query, text_key, text_value, text_grad = (text_own.at[a] for a in range(4))

    self_gate = jnp.where(tile_at == 0, 0.0, NEG).astype(F32)
    gate_query, gate_key = [], []
    for dr in [0, 1 - 2 * row] if hgt_size == 4 else [0, -1, 1]:
        for dc in (0, -1, 1):
            near_row, near_col = row + dr, wid + dc
            inside = (near_row >= 0) & (near_row < tile_rows)
            inside = inside & (near_col >= 0) & (near_col < wid_size)
            near_row = jnp.clip(near_row, 0, tile_rows - 1)
            near_tile = near_row * wid_size + jnp.clip(near_col, 0, wid_size - 1)
            slot = (dr + 1) * 3 + dc + 1
            for gates, entry in (
                (gate_query, windows[tile_at, slot]),
                (gate_key, windows[near_tile, 8 - slot]),
            ):
                gates.append(jnp.where(inside & (entry >= 0), 0.0, NEG).astype(F32))
    pl.semaphore_wait(barrier, devices - 1)
    halves = [
        copy(
            arrays[a].at[:, pl.ds(other, width)],
            tiles.at[a, 0, pl.ds(half, half)],
            half_send.at[a],
            half_recv.at[a],
            mate,
        )
        for a in range(4)
    ]
    for move in halves:
        move.start()

    def hop(a, source, target, device):
        return copy(
            tiles.at[a, source],
            tiles.at[a, target],
            tile_send.at[a, target],
            tile_recv.at[a, target],
            device,
        )

    def stat_hop(source, target, device):
        return copy(
            stats.at[source],
            stats.at[target],
            stat_send.at[target],
            stat_recv.at[target],
            device,
        )

    sent = []

    def launch(make, conds):
        when(conds, lambda: make().start())
        sent.append((make, conds))

    def arrive(make, conds):
        when(conds, lambda: make().wait_recv())

    def upright_hops(a):
        for r, device, go, _ in uprights:
            launch(functools.partial(hop, a, 0, 3 * r, device), [go])

    def side_hops(a):
        for c, device, go, _ in sides:
            launch(functools.partial(hop, a, 0, c, device), [go])

    def routes(a):
        if a == 1:
            return [(True, par == 0), (False, par == 1)]
        return [(a == 2, None)]

    def second_hops(a):
        for by_side_first, use in routes(a):
            if by_side_first:
                for c, device, _, come in sides:
                    arrive(functools.partial(hop, a, 0, c, device), [come, use])
                for r, device, go, _ in uprights:
                    for c, _, _, come in sides:
                        launch(functools.partial(hop, a, c, 3 * r + c, device), [go, come, use])
            else:
                for r, device, _, come in uprights:
                    arrive(functools.partial(hop, a, 0, 3 * r, device), [come, use])
                for r, _, _, come in uprights:
                    for c, device, go, _ in sides:
                        launch(
                            functools.partial(hop, a, 3 * r, 3 * r + c, device), [go, come, use]
                        )

    def direct_arrived(a):
        for by_side_first, use in routes(a):
            if by_side_first:
                for r, device, _, come in uprights:
                    arrive(functools.partial(hop, a, 0, 3 * r, device), [come, use])
            else:
                for c, device, _, come in sides:
                    arrive(functools.partial(hop, a, 0, c, device), [come, use])

    def corners_arrived(a):
        for r, _, _, come_row in uprights:
            for c, device, _, come in sides:
                arrive(lambda: hop(a, 0, 3 * r + c, device), [come, come_row])

    def clear(slot, conds):
        def run():
            for a in range(4):
                tiles[a, slot] = jnp.zeros((size, width), BF16)
            stats[slot] = jnp.zeros(stats.shape[1:], F32)

        neither(conds, run)

    for a in range(4):
        loads[a].wait()
        halves[a].wait_recv()
        if a < 2:
            upright_hops(a)
            side_hops(a)
    for c, _, _, come in sides:
        clear(c, [come])
    for r, _, _, come_row in uprights:
        clear(3 * r, [come_row])
        for c, _, _, come in sides:
            clear(3 * r + c, [come, come_row])

    def lanes(h):
        return pl.ds(pl.multiple_of(h * D, D), D)

    for load in text_loads:
        load.wait()

    def out_lanes(h):
        return pl.ds(pl.multiple_of(mine + h * D, D), D)

    def text_scores(h):
        query, grad = text_query[:, lanes(h)], text_grad[:, lanes(h)]
        near = dot_nt(tiles[0, 0, :, lanes(h)], query) * SCALE
        own = dot_nt(text_key[:, lanes(h)], query) * SCALE + (text_bias[...] + self_gate)
        dp_near = dot_nt(tiles[1, 0, :, lanes(h)], grad)
        dp_own = dot_nt(text_value[:, lanes(h)], grad)
        return query, grad, near, own, dp_near, dp_own

    @pl.loop(0, heads)
    def _(h):
        _, _, near, own, dp_near, dp_own = text_scores(h)
        top = jnp.maximum(
            jnp.max(near, axis=0, keepdims=True), jnp.max(own, axis=0, keepdims=True)
        )
        e_near = jnp.exp(near - top)
        e_own = jnp.exp(own - top)
        total = jnp.sum(e_near, axis=0, keepdims=True) + jnp.sum(e_own, axis=0, keepdims=True)
        mix = jnp.sum(e_near * dp_near, axis=0, keepdims=True) + jnp.sum(
            e_own * dp_own, axis=0, keepdims=True
        )
        text_stats[0, h] = jnp.concatenate(
            [top, total, mix, jnp.zeros((5, top.shape[1]), F32)], axis=0
        )

    def text_copy(step):
        return copy(
            text_stats.at[0],
            text_stats.at[step],
            text_send.at[step],
            text_recv.at[step],
            tile_peer(step),
        )

    @pl.loop(1, tile_count)
    def _(step):
        text_copy(step).start()

    second_hops(0)
    second_hops(1)
    upright_hops(2)
    side_hops(2)
    upright_hops(3)

    @pl.loop(1, tile_count)
    def _(step):
        text_copy(step).wait_recv()

    def spread(at, h, value):
        text_parts[:, at, :, lanes(h)] = value.reshape(text // grain, grain, D).astype(BF16)

    @pl.loop(0, heads)
    def _(h):
        query, grad, near, own, dp_near, dp_own = text_scores(h)
        parts = text_stats[:, h]
        tops = parts[:, 0, :]
        top = jnp.max(tops, axis=0, keepdims=True)
        factor = jnp.exp(tops - top)
        total = jnp.sum(parts[:, 1, :] * factor, axis=0, keepdims=True)
        delta = jnp.sum(parts[:, 2, :] * factor, axis=0, keepdims=True) / total
        lse = top + jnp.log(total)
        p_near = jnp.exp(near - lse)
        p_own = jnp.exp(own - lse)
        low_near = p_near.astype(BF16)
        low_own = p_own.astype(BF16)
        ds_near = (p_near * (dp_near - delta)).astype(BF16)
        ds_own = (p_own * (dp_own - delta)).astype(BF16)
        spread(
            0,
            h,
            dot_tn(low_near, tiles[1, 0, :, lanes(h)])
            + dot_tn(low_own, text_value[:, lanes(h)]),
        )
        spread(
            1,
            h,
            dot_tn(ds_near, tiles[0, 0, :, lanes(h)]) + dot_tn(ds_own, text_key[:, lanes(h)]),
        )
        self_keys[0, :, lanes(h)] = dot_nn(ds_own, query)
        self_keys[1, :, lanes(h)] = dot_nn(low_own, grad)
        near_keys[0, :, lanes(h)] = dot_nn(ds_near, query)
        near_keys[1, :, lanes(h)] = dot_nn(low_near, grad)

    for a in range(2):
        direct_arrived(a)
    for a in range(2):
        corners_arrived(a)
    side_hops(3)
    second_hops(3)

    spans = [(at * size, size) for at in range(count)] + [(count * size, text)]

    @pl.loop(0, heads)
    def _(h):
        @pl.when(h == heads // 2)
        def _():
            second_hops(2)

        query, grad = tiles[2, 0, :, lanes(h)], tiles[3, 0, :, lanes(h)]

        def key_of(at):
            return tiles[0, at, :, lanes(h)] if at < count else text_key[:, lanes(h)]

        def value_of(at):
            return tiles[1, at, :, lanes(h)] if at < count else text_value[:, lanes(h)]

        top = None
        for at, (first, length) in enumerate(spans):
            part = dot_nt(key_of(at), query) * SCALE
            part = part + (gate_query[at] if at < count else text_bias[...][:, :1])
            score[first : first + length] = part
            peak = jnp.max(part, axis=0, keepdims=True)
            top = peak if top is None else jnp.maximum(top, peak)
        shift = round_bf16(top)
        total = jnp.zeros_like(shift)
        for first, length in spans:
            weight = jnp.exp(score[first : first + length] - shift)
            score[first : first + length] = weight
            total = total + jnp.sum(weight, axis=0, keepdims=True)
        inverse = round_bf16(1.0 / total)
        out = jnp.zeros((D, size), F32)
        for at, (first, length) in enumerate(spans):
            low = (score[first : first + length] * inverse).astype(BF16)
            out = out + dot_tn(value_of(at), low)
            if at == count:
                spread(3, h, self_keys[1, :, lanes(h)] + dot_nn(low, grad))
        out = round_bf16(out)
        delta = round_bf16(jnp.sum(grad.astype(F32).T * out, axis=0, keepdims=True))
        query_grad = jnp.zeros((D, size), F32)
        for at, (first, length) in enumerate(spans):
            dp = dot_nt(value_of(at), grad)
            ds = (score[first : first + length] * inverse * (dp - delta)).astype(BF16)
            query_grad = query_grad + dot_tn(key_of(at), ds)
            if at == count:
                spread(2, h, self_keys[0, :, lanes(h)] + dot_nn(ds, query))
        for at, value in enumerate((out.T, (query_grad * SCALE).T)):
            value = value.astype(BF16)
            outs[at][:, out_lanes(h)] = value[:half]
            back[at, :, lanes(h)] = value[half:]
        stats[0, h] = jnp.concatenate([shift, inverse, delta, jnp.zeros((5, size), F32)], axis=0)

    for r, device, go, _ in uprights:
        launch(functools.partial(stat_hop, 0, 3 * r, device), [go])
    for c, device, go, _ in sides:
        launch(functools.partial(stat_hop, 0, c, device), [go])

    def part_copy(step):
        peer, device = rank_peer(step)
        return copy(
            text_parts.at[peer * owned // grain],
            text_landed.at[step],
            part_send.at[step],
            part_recv.at[step],
            device,
        )

    @pl.loop(1, devices)
    def _(step):
        part_copy(step).start()

    def back_copy(at):
        return copy(back.at[at], landed.at[at], back_send.at[at], back_recv.at[at], mate)

    for at in range(2):
        back_copy(at).start()

    for r, device, _, come in uprights:
        arrive(lambda: stat_hop(0, 3 * r, device), [come])
    for r, _, _, come in uprights:
        for c, device, go, _ in sides:
            launch(functools.partial(stat_hop, 3 * r, 3 * r + c, device), [go, come])
    for c, device, _, come in sides:
        arrive(lambda: stat_hop(0, c, device), [come])
    direct_arrived(2)
    direct_arrived(3)

    def key_part(h, slots):
        key, value = tiles[0, 0, :, lanes(h)], tiles[1, 0, :, lanes(h)]
        key_grad = near_keys[0, :, lanes(h)]
        value_grad = near_keys[1, :, lanes(h)]
        for at in slots:
            query, grad = tiles[2, at, :, lanes(h)], tiles[3, at, :, lanes(h)]
            rows = stats[at, h]
            shift, inverse, delta = rows[0:1], rows[1:2], rows[2:3]
            prob = jnp.exp(dot_nt(key, query) * SCALE + (gate_key[at] - shift)) * inverse
            ds = (prob * (dot_nt(value, grad) - delta)).astype(BF16)
            value_grad = value_grad + dot_nn(prob.astype(BF16), grad)
            key_grad = key_grad + dot_nn(ds, query)
        return key_grad, value_grad

    corners = [3 * r + c for r, _, _, _ in uprights for c in (1, 2)]

    @pl.loop(0, heads)
    def _(h):
        key_grad, value_grad = key_part(h, [at for at in range(count) if at not in corners])
        near_keys[0, :, lanes(h)] = key_grad
        near_keys[1, :, lanes(h)] = value_grad

    for r, _, _, come_row in uprights:
        for c, device, _, come in sides:
            arrive(lambda: stat_hop(0, 3 * r + c, device), [come, come_row])
    corners_arrived(2)
    corners_arrived(3)

    @pl.loop(0, heads)
    def _(h):
        key_grad, value_grad = key_part(h, corners)
        for at, grads in ((2, key_grad * SCALE), (3, value_grad)):
            grads = grads.astype(BF16)
            outs[at][:, out_lanes(h)] = grads[:half]
            back[at, :, lanes(h)] = grads[half:]

    for at in range(2, 4):
        back_copy(at).start()

    @pl.loop(1, devices)
    def _(step):
        part_copy(step).wait_recv()

    own_part = text_parts[rank * owned // grain].astype(F32)

    def add_pair(step, sums):
        same = sums[0] + text_landed[2 * step].astype(F32)
        return same, sums[1] + text_landed[2 * step + 1].astype(F32)

    same, cross = lax.fori_loop(
        1, devices // 2, add_pair, (own_part, text_landed[1].astype(F32))
    )
    text_out[:, :, pl.ds(mine, width)] = same
    text_out[:, :, pl.ds(other, width)] = cross

    for at in range(4):
        back_copy(at).wait_recv()
        outs[at][:, pl.ds(other, width)] = landed[at]

    for move in halves:
        move.wait_send()
    for make, conds in sent:
        when(conds, lambda: make().wait_send())

    @pl.loop(1, tile_count)
    def _(step):
        text_copy(step).wait_send()

    @pl.loop(1, devices)
    def _(step):
        part_copy(step).wait_send()

    for at in range(4):
        back_copy(at).wait_send()


def finish_kernel(owned, grain, hgt_size, *refs):
    ins, text_sums = refs[:4], refs[4]
    outs, text_outs = refs[5:9], refs[9:13]
    for a in range(4):
        outs[a][...] = ins[a][...]
    rank = lax.axis_index("wid") * hgt_size + lax.axis_index("hgt")
    first = 0 if owned == grain else lax.rem(rank * owned, grain)
    for a in range(4):
        sums = text_sums[a, pl.ds(first, owned), :]
        text_outs[a][...] = (sums * SCALE if a in (1, 2) else sums).astype(BF16)


def per_device(
    latent_query,
    latent_key,
    latent_value,
    latent_grad,
    text_query,
    text_key,
    text_value,
    text_grad,
    text_valid,
    windows,
):
    block = latent_query.shape
    channels = block[3]
    rows = block[0] * block[1] * block[2]
    size = 2 * rows
    width = channels // 2
    heads = width // D
    text = text_query.shape[0]
    wid_size, hgt_size = lax.axis_size("wid"), lax.axis_size("hgt")
    devices = wid_size * hgt_size
    count = 6 if hgt_size == 4 else 9
    text_bias = jnp.broadcast_to(
        jnp.where(text_valid == 1, 0.0, NEG).astype(F32)[:, None], (text, text)
    )
    owned = text // devices
    grain = max(owned, 8)
    flat = [a.reshape(rows, channels) for a in (latent_key, latent_value, latent_query, latent_grad)]
    smem = pl.BlockSpec(memory_space=pltpu.SMEM)
    hbm = pl.BlockSpec(memory_space=pl.ANY)
    vmem = pl.BlockSpec(memory_space=pltpu.VMEM)
    dma = pltpu.SemaphoreType.DMA
    whole = jax.ShapeDtypeStruct((rows, channels), BF16)
    results = pl.pallas_call(
        functools.partial(whole_kernel, wid_size, hgt_size),
        in_specs=[smem] + [hbm] * 8 + [vmem],
        out_specs=[vmem] * 5,
        out_shape=[whole] * 4 + [jax.ShapeDtypeStruct((4, grain, channels), F32)],
        scratch_shapes=[
            pltpu.VMEM((4, count, size, width), BF16),
            pltpu.VMEM((4, text, width), BF16),
            pltpu.VMEM((count * size + text, size), F32),
            pltpu.VMEM((count, heads, 8, size), F32),
            pltpu.VMEM((devices // 2, heads, 8, text), F32),
            pltpu.VMEM((2, size, width), F32),
            pltpu.VMEM((2, text, width), F32),
            pltpu.VMEM((text // grain, 4, grain, width), BF16),
            pltpu.VMEM((devices, 4, grain, width), BF16),
            pltpu.VMEM((4, rows, width), BF16),
            pltpu.VMEM((4, rows, width), BF16),
            dma((4,)),
            dma((4,)),
            dma((4,)),
            dma((4,)),
            dma((4, count)),
            dma((4, count)),
            dma((count,)),
            dma((count,)),
            dma((devices // 2,)),
            dma((devices // 2,)),
            dma((devices,)),
            dma((devices,)),
            dma((4,)),
            dma((4,)),
        ],
        compiler_params=pltpu.CompilerParams(
            collective_id=0, has_side_effects=True, vmem_limit_bytes=56 * 1024 * 1024
        ),
        name="joint_attention",
    )(windows, *flat, text_query, text_key, text_value, text_grad, text_bias)
    finished = pl.pallas_call(
        functools.partial(finish_kernel, owned, grain, hgt_size),
        in_specs=[vmem] * 5,
        out_specs=[vmem] * 8,
        out_shape=[whole] * 4 + [jax.ShapeDtypeStruct((owned, channels), BF16)] * 4,
        name="finish",
    )(*results)
    return tuple([a.reshape(block) for a in finished[:4]] + list(finished[4:]))


def solution(mesh):
    tiles = P("grp", "hgt", "wid", None)
    rows = P(("grp", "wid", "hgt"), None)
    return jax.shard_map(
        per_device,
        mesh=mesh,
        in_specs=(tiles,) * 4 + (P("grp", None),) * 4 + (P("grp"), P()),
        out_specs=(tiles,) * 4 + (rows,) * 4,
        check_vma=False,
    )
```
